1024 devices in a mesh: rep: 32 (over x, y, z_hi), grp: 32 (over z_lo, core).
Axes of the slice: x: 4, y: 4, z: 32 (z_hi: 2, z_lo: 16; z = z_hi * 16 + z_lo), core: 2. Of those that a mesh axis runs over, the one named last changes fastest.
Arguments:
- activations: bfloat16 [524288, 512], P(('rep', 'grp')), may hold values from -6 to 6
- out_grads: bfloat16 [524288, 1024], P(('rep', 'grp')), may hold values from -0.0014648438 to 0.0014648438
- stats_old: float32 [4, 512, 512], P(None, 'grp'), as said below
Outputs:
- stats_new: float32 [4, 512, 512], P(None, 'grp')
- update: float32 [2, 512, 512], P(None, 'grp')
The draws below stay inside these ranges and needn't reach their ends.
Inputs may be any that keep to these rules, and one draw needn't show every extreme that they name: Each stats_old[c] is symmetric positive definite.
All inputs are finite; a program needn't handle non-finite values.
Results may differ from the reference program's by a relative error of at most 0.0009.
The reference program's roundings to bfloat16 on the way count: a program that leaves them out, or rounds other values in their place, can miss the bound.
Values may be sent and summed in bfloat16 or wider, within the bound.
A program may use at most 32 MiB of HBM per device.

```python
import math
import jax
import jax.numpy as jnp
from jax import lax

BLK = 512
TILES = 2
ITERS = 2
TOKENS = 524288


def draw_stats_old(key, part):
    key_base = jax.random.fold_in(key, 11)
    key_jitter = jax.random.fold_in(key, 12)
    base = jax.random.normal(key_base, (2 * TILES, BLK, BLK), jnp.float32)
    spread = math.log(3.0)
    gram = jnp.einsum('cij,ckj->cik', base, base) / BLK + jnp.eye(BLK, dtype=jnp.float32)
    jitter = jax.random.uniform(key_jitter, (2 * TILES, BLK), jnp.float32, -0.35, 0.35)
    rising = jnp.arange(BLK, dtype=jnp.float32) / BLK * spread
    scales = jnp.exp(rising[None, :] + jitter)
    return gram * scales[:, :, None] * scales[:, None, :]


def spiked(values, key, source, target, shards_of, factor):
    def block_of(dim):
        return (jnp.arange(values.shape[dim]) // (values.shape[dim] // shards_of)).reshape((-1,) + (1,) * (values.ndim - 1 - dim))

    near = jax.random.permutation(key, shards_of)[block_of(target)]
    second = (block_of(target) + shards_of // 2) % shards_of
    return jnp.where((block_of(source) == near) | (block_of(source) == second), factor * values, values)


def block_scale(rng, dims, shards, least, largest):
    gain = 1.0
    for axis_at, parts in shards:
        draws = jax.random.uniform(jax.random.fold_in(jax.random.fold_in(rng, 6), axis_at), (parts,), jnp.float32, least / len(shards), largest / len(shards))
        gain = gain * jnp.repeat(jnp.exp(draws), dims[axis_at] // parts).reshape((-1,) + (1,) * (len(dims) - 1 - axis_at))
    return gain


def scatter_about(stream_key, shape, width, most, cuts=(), kind=jnp.bfloat16):
    loudness = block_scale(stream_key, shape, cuts, -0.22, 0.18) if cuts else 1.0
    array = jax.random.normal(stream_key, shape, jnp.float32) * width * loudness
    return jnp.minimum(jnp.maximum(array, -most), most).astype(kind)


def gaussian_with(key, dims, scale, most, split, heavy, kind=jnp.bfloat16):
    result = scale * jax.random.normal(key, dims, jnp.float32)
    if split:
        result = result * block_scale(key, dims, split, -0.22, 0.18)
    return jnp.clip(spiked(result, jax.random.fold_in(key, 3), *heavy), -most, most).astype(kind)


def setup_inputs(seed: int = 0) -> dict:
    arg_keys = jax.random.split(jax.random.key(seed), 4)
    return {
        "activations": scatter_about(arg_keys[0], (TOKENS, BLK), 1.0, 6.0, ((0, 1024),)),
        "out_grads": gaussian_with(arg_keys[1], (TOKENS, TILES * BLK), (TOKENS * BLK) ** -0.5, 0.0014648438, ((0, 1024),), (0, 1, 1024, 6.0)),
        "stats_old": draw_stats_old(jax.random.fold_in(arg_keys[3], 71), 0),
    }


DAMPING = 0.01

def newton_root(damped):
    order_size = damped.shape[0]
    identity = jnp.eye(order_size, dtype=jnp.float32)
    scale = 2.5 / jnp.sqrt(jnp.sum(damped * damped))
    iterate = scale * damped
    factors = []
    for iteration in range(ITERS):
        factor = ((5.0 * identity - iterate) * 0.25).astype(jnp.bfloat16)
        factors.append(factor)
        if iteration + 1 < ITERS:
            upcast = factor.astype(jnp.float32)
            for repeat in range(4):
                iterate = jnp.dot(iterate, upcast, precision=lax.Precision.HIGHEST)
    if len(factors) == 1:
        running = factors[0].astype(jnp.float32)
    else:
        running = jnp.dot(factors[0], factors[1], preferred_element_type=jnp.float32)
        for later in factors[2:]:
            running = jnp.dot(running, later.astype(jnp.float32), precision=lax.Precision.HIGHEST)
    return (scale ** 0.25 * running).astype(jnp.bfloat16)

def reference(activations, out_grads, stats_old):
    token_total = activations.shape[0]
    block_rows = math.gcd(token_total, 4096)
    block_count = token_total // block_rows

    def accumulate(carry, index):
        first_row = (index * block_rows).astype(jnp.int32)
        inputs = lax.dynamic_slice_in_dim(activations, first_row, block_rows, 0)
        grads = lax.dynamic_slice_in_dim(out_grads, first_row, block_rows, 0)
        return (carry + jnp.dot(grads.T, inputs, preferred_element_type=jnp.float32), None)
    summed, _ = lax.scan(accumulate, jnp.zeros((TILES * BLK, BLK), jnp.float32), jnp.arange(block_count, dtype=jnp.int32))
    gradient = summed.astype(jnp.bfloat16).reshape(TILES, BLK, BLK)
    left_terms = [jnp.dot(gradient[tile].T, gradient[tile], preferred_element_type=jnp.float32) for tile in range(TILES)]
    right_terms = [jnp.dot(gradient[tile], gradient[tile].T, preferred_element_type=jnp.float32) for tile in range(TILES)]
    stats_new = stats_old + jnp.stack(left_terms + right_terms)
    identity = jnp.eye(BLK, dtype=jnp.float32)
    roots = [newton_root(stats_new[chain] + DAMPING * identity) for chain in range(2 * TILES)]
    updates = []
    for tile in range(TILES):
        inner_rows = jnp.dot(roots[TILES + tile], gradient[tile], preferred_element_type=jnp.float32)
        updates.append(jnp.dot(inner_rows, roots[tile].astype(jnp.float32), precision=lax.Precision.HIGHEST) * math.sqrt(BLK))
    return (stats_new, jnp.stack(updates))
```

```python
import functools
import math

import jax
import jax.numpy as jnp
from jax import lax
from jax.experimental import pallas as pl
from jax.experimental.pallas import tpu as pltpu
from jax.sharding import PartitionSpec as P

MESH = pl.DeviceIdType.MESH
F32 = jnp.float32
BF16 = jnp.bfloat16
DAMPING = 0.01
ITERS = 2


def div(a, b):
    return lax.div(a, jnp.int32(b))


def rem(a, b):
    return lax.rem(a, jnp.int32(b))


def dot(a, b):
    return jnp.dot(a, b, preferred_element_type=F32)


def transposed_dot(a, b):
    return lax.dot_general(a, b, (((0,), (0,)), ((), ())), preferred_element_type=F32)


def copy_to(src, dst, send, recv, device):
    return pltpu.make_async_remote_copy(
        src_ref=src, dst_ref=dst, send_sem=send, recv_sem=recv, device_id=device, device_id_type=MESH
    )


def kernel(
    act, og, old, stats, update,
    act_v, og_v, old_v, acc, got0, got1, got2, got3, shard, parts, blocks, pieces, grad, grad_t,
    column, planes, old_full, new_full, factor0, factor1, split, root, upd, upd_got,
    load_sem, core_send, core_recv, sum_send, sum_recv, part_send, part_recv, block_send, block_recv,
    piece_send, piece_recv, grad_send, grad_recv, near_sem, far_send, far_recv, col_send, col_recv,
    plane_send, plane_recv, out_sem, out_send, out_recv, know,
):
    rep, grp = lax.axis_index("rep"), lax.axis_index("grp")
    z_hi, xy = rem(rep, 2), div(rep, 2)
    y, x = rem(xy, 4), div(xy, 4)
    core, z_lo = rem(grp, 2), div(grp, 2)
    z = z_hi * 16 + z_lo
    blk, pos = div(z, 8), rem(z, 8)
    other = 1 - core

    def device(x_at, y_at, z_at, core_at):
        return {"rep": (x_at * 4 + y_at) * 2 + div(z_at, 16), "grp": rem(z_at, 16) * 2 + core_at}

    def along(k):
        return device(x, y, rem(z + (k + 32), 32), core)

    def in_block(k):
        return device(x, y, blk * 8 + rem(pos + k, 8), core)

    partner = device(x, y, z, other)
    hops = [
        device(x + 1 - 2 * rem(x, 2), y, z, core),
        device(3 - x, y, z, core),
        device(x, y + 1 - 2 * rem(y, 2), z, core),
        device(x, 3 - y, z, core),
    ]
    bits = [rem(rem(x, 2) + div(x, 2), 2), div(x, 2), rem(rem(y, 2) + div(y, 2), 2), div(y, 2)]
    twin = device(x, y, z_hi * 16 + rem(z_lo + 8, 16), core)

    own_cols = pl.ds(pl.multiple_of(core * 512, 512), 512)
    other_cols = pl.ds(pl.multiple_of(other * 512, 512), 512)
    loads = [
        pltpu.make_async_copy(act, act_v.at[0], load_sem.at[0]),
        pltpu.make_async_copy(og.at[:, own_cols], og_v.at[0], load_sem.at[1]),
        pltpu.make_async_copy(old.at[core], old_v.at[core, 0], load_sem.at[2]),
        pltpu.make_async_copy(old.at[core + 2], old_v.at[core, 1], load_sem.at[3]),
    ]
    for load in loads:
        load.start()

    barrier = pltpu.get_barrier_semaphore()
    for near in [partner, *hops, along(1), along(-1)]:
        pl.semaphore_signal(barrier, inc=1, device_id=near, device_id_type=MESH)
    pl.semaphore_wait(barrier, 7)

    def spread(k):
        for far in (along(1 << k), along(-(1 << k))):
            pl.semaphore_signal(know.at[k], inc=1, device_id=far, device_id_type=MESH)

    swaps = [
        copy_to(og.at[:, other_cols], og_v.at[1], core_send.at[0], core_recv.at[0], partner),
        copy_to(act, act_v.at[1], core_send.at[1], core_recv.at[1], partner),
        copy_to(old.at[other], old_v.at[core, 0], core_send.at[2], core_recv.at[2], partner),
        copy_to(old.at[other + 2], old_v.at[core, 1], core_send.at[3], core_recv.at[3], partner),
    ]
    for swap in swaps:
        swap.start()
    spread(0)

    def local_term(side, add):
        def body(m, carry):
            rows = pl.ds(pl.multiple_of(m * 128, 128), 128)
            term = transposed_dot(og_v[side, :, rows], act_v[side])
            for q in range(4):
                value = term[:, q * 128 : (q + 1) * 128]
                acc[q, rows, :] = acc[q, rows, :] + value if add else value
            return carry

        lax.fori_loop(0, 4, body, 0)

    for load in loads:
        load.wait()
    local_term(0, False)
    pl.semaphore_wait(know.at[0], 2)
    spread(1)
    swaps[0].wait_recv()
    swaps[1].wait_recv()
    local_term(1, True)

    got = [got0, got1, got2, got3]
    base = [jnp.int32(0)] * 4
    sums = []

    def send_sum(k, q):
        size = 256 >> k
        d = (q + k) % 4
        away = pl.multiple_of(base[q] + size * (1 - bits[d]), size)
        base[q] = base[q] + size * bits[d]
        copy = copy_to(
            acc.at[q, pl.ds(away, size)], got[k].at[q], sum_send.at[k, q], sum_recv.at[k, q], hops[d]
        )
        copy.start()
        sums.append(copy)

    def take_sum(k, q):
        size = 256 >> k
        sums[k * 4 + q].wait_recv()
        keep = pl.ds(pl.multiple_of(base[q], size), size)
        return acc[q, keep, :] + got[k][q], keep

    for q in range(4):
        send_sum(0, q)
    pl.semaphore_wait(know.at[1], 2)
    spread(2)
    swaps[2].wait_recv()
    swaps[3].wait_recv()

    slice_cols = pl.ds(pl.multiple_of((bits[2] * 2 + bits[3]) * 128, 128), 128)
    mine = old_v.at[bits[1], bits[0], :, slice_cols]
    half = div(z_lo, 8)
    stage = pltpu.make_async_copy(mine, column.at[pos, half], near_sem.at[0])
    stage.start()
    for k in range(1, 4):
        if k == 2:
            pl.semaphore_wait(know.at[2], 2)
            spread(3)
            far = copy_to(mine, column.at[pos, half], far_send.at[0], far_recv.at[0], twin)
            far.start()
        for q in range(4):
            value, keep = take_sum(k - 1, q)
            acc[q, keep, :] = value
            send_sum(k, q)
    stage.wait()
    for q in range(4):
        value, keep = take_sum(3, q)
        for h in range(2):
            shard[2 * q + h] = value[16 * h : 16 * h + 16]

    to_parts = []
    for k in range(1, 8):
        copy = copy_to(
            shard.at[rem(pos + k, 8)], parts.at[k - 1], part_send.at[k - 1], part_recv.at[k - 1], in_block(k)
        )
        copy.start()
        to_parts.append(copy)

    far.wait_recv()
    columns = []
    for k in range(1, 8):
        copy = copy_to(column.at[pos], column.at[pos], col_send.at[k - 1], col_recv.at[k - 1], in_block(k))
        copy.start()
        columns.append(copy)
    for copy in columns:
        copy.wait_recv()

    number = bits[0] + 2 * bits[1] + 4 * bits[2] + 8 * bits[3]
    slots = [div(number, 1 << r) + rem(number, 1 << r) * (1 << (4 - r)) for r in range(4)]
    stages = [
        pltpu.make_async_copy(column.at[pl.ds(2 * r, 2)], planes.at[r, slots[r]], near_sem.at[1 + r])
        for r in range(4)
    ]
    for copy in stages:
        copy.start()
    for copy in stages:
        copy.wait()
    spreads = []

    def send_plane(k):
        for r in range(4):
            size = 1 << k
            first = pl.ds(slots[r] - rem(slots[r], size), size)
            copy = copy_to(
                planes.at[r, first], planes.at[r, first], plane_send.at[k, r], plane_recv.at[k, r], hops[(r + k) % 4]
            )
            copy.start()
            spreads.append(copy)

    def take_plane(k):
        for r in range(4):
            spreads[4 * k + r].wait_recv()

    send_plane(0)
    take_plane(0)
    send_plane(1)

    total = shard[pos]
    for k in range(1, 8):
        to_parts[k - 1].wait_recv()
        total = total + parts[k - 1]
    blocks[blk] = total
    pl.semaphore_wait(know.at[3], 2)
    to_blocks = []
    for k in range(1, 4):
        copy = copy_to(
            blocks.at[blk], blocks.at[blk], block_send.at[k - 1], block_recv.at[k - 1], along(8 * k)
        )
        copy.start()
        to_blocks.append(copy)

    take_plane(1)
    send_plane(2)
    take_plane(2)
    send_plane(3)
    take_plane(3)

    for r in range(4):

        def lay(slot, carry):
            bit = [rem(div(slot, 1 << ((d - r) % 4)), 2) for d in range(4)]
            quarter = bit[2] * 2 + bit[3]
            for b in range(2):
                for a in range(2):
                    first = pl.multiple_of((a * 8 + 2 * r + b) * 32 + bit[1] * 16, 16)
                    old_full[bit[0], quarter, pl.ds(first, 16), :] = planes[r, slot, b, a]
            return carry

        lax.fori_loop(0, 16, lay, 0)

    for copy in to_blocks:
        copy.wait_recv()
    pieces[pos] = (((blocks[0] + blocks[1]) + blocks[2]) + blocks[3]).astype(BF16)
    to_pieces = []
    for k in range(1, 8):
        copy = copy_to(pieces.at[pos], pieces.at[pos], piece_send.at[k - 1], piece_recv.at[k - 1], in_block(k))
        copy.start()
        to_pieces.append(copy)
    for copy in to_pieces:
        copy.wait_recv()

    for q in range(4):
        for h in range(2):
            first = pl.multiple_of(base[q] + 16 * h, 16)
            grad[pl.ds(first, 16), q * 128 : (q + 1) * 128] = pieces[2 * q + h]
    gathers = []
    for k in range(3, -1, -1):
        size = 256 >> k
        for q in range(4):
            d = (q + k) % 4
            if k < 3:
                gathers[(2 - k) * 4 + q].wait_recv()
            rows = pl.ds(pl.multiple_of(base[q], size), size)
            part = grad.at[rows, q * 128 : (q + 1) * 128]
            copy = copy_to(part, part, grad_send.at[k, q], grad_recv.at[k, q], hops[d])
            copy.start()
            gathers.append(copy)
            base[q] = base[q] - size * bits[d]
    for copy in gathers[12:]:
        copy.wait_recv()

    def eye_of(m):
        row = lax.broadcasted_iota(jnp.int32, (128, 512), 0) + m * 128
        return (row == lax.broadcasted_iota(jnp.int32, (128, 512), 1)).astype(F32)

    def flip(m, carry):
        rows = pl.ds(pl.multiple_of(m * 128, 128), 128)
        grad_t[rows, :] = grad[:, rows].T
        return carry

    lax.fori_loop(0, 4, flip, 0)

    def gram(m, carry):
        rows = pl.ds(pl.multiple_of(m * 128, 128), 128)
        eye = eye_of(m)
        sums_now = []
        for chain in range(2):
            left, right = (grad_t, grad) if chain == 0 else (grad, grad_t)
            term = dot(left[rows, :], right[...])
            quarters = [old_full[chain, q, rows, :] for q in range(4)]
            value = jnp.concatenate(quarters, axis=1) + term
            new_full[chain, rows, :] = value
            damped = value + DAMPING * eye
            sums_now.append(carry[chain] + jnp.sum(damped * damped, axis=0, keepdims=True))
        return tuple(sums_now)

    zero = jnp.zeros((1, 512), F32)
    squares = lax.fori_loop(0, 4, gram, (zero, zero))
    own_first = pl.multiple_of(z_lo * 32 + 16 * core, 16)
    other_first = pl.multiple_of(z_lo * 32 + 16 * other, 16)
    outs, sends = [], []
    for chain in range(2):
        outs.append(
            pltpu.make_async_copy(
                new_full.at[chain, pl.ds(own_first, 16)], stats.at[2 * chain + core], out_sem.at[chain]
            )
        )
        sends.append(
            copy_to(
                new_full.at[chain, pl.ds(other_first, 16)], stats.at[2 * chain + core],
                out_send.at[chain], out_recv.at[chain], partner,
            )
        )
        outs[-1].start()
        sends[-1].start()

    scales = [2.5 / jnp.sqrt(jnp.sum(part, axis=1, keepdims=True)) for part in squares]
    quarters = [jnp.sqrt(jnp.sqrt(scale)) for scale in scales]

    def begin(m, carry):
        rows = pl.ds(pl.multiple_of(m * 128, 128), 128)
        eye = eye_of(m)
        for chain in range(2):
            iterate = scales[chain] * (new_full[chain, rows, :] + DAMPING * eye)
            factor0[chain, rows, :] = ((5.0 * eye - iterate) * 0.25).astype(BF16)
            high = iterate.astype(BF16)
            split[chain, 0, rows, :] = high
            split[chain, 1, rows, :] = (iterate - high.astype(F32)).astype(BF16)
        return carry

    lax.fori_loop(0, 4, begin, 0)

    def multiply(step, carry):
        for top in range(2):
            rows = slice(256 * top, 256 * top + 256)
            for chain in range(2):
                whole = factor0[chain]
                iterate = dot(split[chain, 0, rows, :], whole) + dot(split[chain, 1, rows, :], whole)
                high = iterate.astype(BF16)
                split[chain, 0, rows, :] = high
                split[chain, 1, rows, :] = (iterate - high.astype(F32)).astype(BF16)
        return carry

    lax.fori_loop(0, 3, multiply, 0)

    row_ids = lax.broadcasted_iota(jnp.int32, (256, 512), 0)
    column_ids = lax.broadcasted_iota(jnp.int32, (256, 512), 1)
    for top in range(2):
        rows = slice(256 * top, 256 * top + 256)
        eye = (row_ids + 256 * top == column_ids).astype(F32)
        for chain in range(2):
            whole = factor0[chain]
            iterate = dot(split[chain, 0, rows, :], whole) + dot(split[chain, 1, rows, :], whole)
            factor1[chain, rows, :] = ((5.0 * eye - iterate) * 0.25).astype(BF16)

    chip_rows = pl.ds(pl.multiple_of(z_lo * 32, 32), 32)
    right_root = (quarters[1] * dot(factor0[1, chip_rows, :], factor1[1])).astype(BF16)
    for top in range(2):
        rows = slice(256 * top, 256 * top + 256)
        root[rows, :] = (quarters[0] * dot(factor0[0, rows, :], factor1[0])).astype(BF16)
    inner = dot(right_root, grad[...])
    high = inner.astype(BF16)
    rest = inner - high.astype(F32)
    middle = rest.astype(BF16)
    low = (rest - middle.astype(F32)).astype(BF16)
    left_root = root[...]
    total = (dot(low, left_root) + dot(middle, left_root)) + dot(high, left_root)
    upd[...] = total * math.sqrt(512)
    outs.append(
        pltpu.make_async_copy(
            upd.at[pl.ds(pl.multiple_of(16 * core, 16), 16)], update.at[core], out_sem.at[2]
        )
    )
    sends.append(
        copy_to(
            upd.at[pl.ds(pl.multiple_of(16 * other, 16), 16)], update.at[core],
            out_send.at[2], out_recv.at[2], partner,
        )
    )
    outs[-1].start()
    sends[-1].start()

    for copy in outs:
        copy.wait()
    for copy in [*swaps, *sums, far, *to_parts, *columns, *spreads, *to_blocks, *to_pieces, *gathers, *sends]:
        copy.wait_send()
    for copy in sends:
        copy.wait_recv()


def on_device(activations, out_grads, stats_old):
    dma = pltpu.SemaphoreType.DMA
    vmem = pltpu.VMEM
    anywhere = pl.BlockSpec(memory_space=pl.ANY)
    return pl.pallas_call(
        kernel,
        out_shape=(
            jax.ShapeDtypeStruct((4, 16, 512), F32),
            jax.ShapeDtypeStruct((2, 16, 512), F32),
        ),
        in_specs=[anywhere] * 3,
        out_specs=(anywhere, anywhere),
        scratch_shapes=[
            vmem((2, 512, 512), BF16),
            vmem((2, 512, 512), BF16),
            vmem((2, 2, 16, 512), F32),
            vmem((4, 512, 128), F32),
            vmem((4, 256, 128), F32),
            vmem((4, 128, 128), F32),
            vmem((4, 64, 128), F32),
            vmem((4, 32, 128), F32),
            vmem((8, 16, 128), F32),
            vmem((7, 16, 128), F32),
            vmem((4, 16, 128), F32),
            vmem((8, 16, 128), BF16),
            vmem((512, 512), BF16),
            vmem((512, 512), BF16),
            vmem((8, 2, 16, 128), F32),
            vmem((4, 16, 2, 2, 16, 128), F32),
            vmem((2, 4, 512, 128), F32),
            vmem((2, 512, 512), F32),
            vmem((2, 512, 512), BF16),
            vmem((2, 512, 512), BF16),
            vmem((2, 2, 512, 512), BF16),
            vmem((512, 512), BF16),
            vmem((32, 512), F32),
            vmem((8, 128), F32),
            dma((4,)),
            dma((4,)), dma((4,)),
            dma((4, 4)), dma((4, 4)),
            dma((7,)), dma((7,)),
            dma((3,)), dma((3,)),
            dma((7,)), dma((7,)),
            dma((4, 4)), dma((4, 4)),
            dma((5,)),
            dma((1,)), dma((1,)),
            dma((7,)), dma((7,)),
            dma((4, 4)), dma((4, 4)),
            dma((3,)),
            dma((3,)), dma((3,)),
            pltpu.SemaphoreType.REGULAR((4,)),
        ],
        compiler_params=pltpu.CompilerParams(
            collective_id=0, has_side_effects=True, vmem_limit_bytes=56 * 1024 * 1024
        ),
    )(activations, out_grads, stats_old)


def solution(mesh):
    in_specs = (P(("rep", "grp"), None), P(("rep", "grp"), None), P(None, "grp", None))
    out_specs = (P(None, "grp", None), P(None, "grp", None))
    return jax.shard_map(
        on_device, mesh=mesh, in_specs=in_specs, out_specs=out_specs, check_vma=False
    )
```

```python
import functools
import math

import jax
import jax.numpy as jnp
from jax import lax
from jax.experimental import pallas as pl
from jax.experimental.pallas import tpu as pltpu
from jax.sharding import PartitionSpec as P

MESH = pl.DeviceIdType.MESH
F32 = jnp.float32
BF16 = jnp.bfloat16
DAMPING = 0.01
ITERS = 2


def div(a, b):
    return lax.div(a, jnp.int32(b))


def rem(a, b):
    return lax.rem(a, jnp.int32(b))


def dot(a, b):
    return jnp.dot(a, b, preferred_element_type=F32)


def transposed_dot(a, b):
    return lax.dot_general(a, b, (((0,), (0,)), ((), ())), preferred_element_type=F32)


def copy_to(src, dst, send, recv, device):
    return pltpu.make_async_remote_copy(
        src_ref=src, dst_ref=dst, send_sem=send, recv_sem=recv, device_id=device, device_id_type=MESH
    )


def kernel(
    act, og, old, stats, update,
    act_v, og_v, old_v, acc, got0, got1, shard, parts, blocks, pieces, grad, grad_t,
    column, planes, old_full, new_full, factor0, factor1, split, root, upd,
    load_sem, core_send, core_recv, sum_send, sum_recv, part_send, part_recv, block_send, block_recv,
    piece_send, piece_recv, grad_send, grad_recv, near_sem, col_send, col_recv,
    plane_send, plane_recv, out_sem, out_send, out_recv, know,
):
    rep, grp = lax.axis_index("rep"), lax.axis_index("grp")
    z_hi, xy = rem(rep, 2), div(rep, 2)
    y, x = rem(xy, 4), div(xy, 4)
    core, z_lo = rem(grp, 2), div(grp, 2)
    z = z_hi * 16 + z_lo
    blk, pos = div(z, 8), rem(z, 8)
    other = 1 - core

    def device(x_at, y_at, z_at, core_at):
        return {"rep": (x_at * 4 + y_at) * 2 + div(z_at, 16), "grp": rem(z_at, 16) * 2 + core_at}

    def along(k):
        return device(x, y, rem(z + (k + 32), 32), core)

    partner = device(x, y, z, other)
    x_at = [x + 1 - 2 * rem(x, 2), 3 - x]
    y_at = [y + 1 - 2 * rem(y, 2), 3 - y]
    bits = [rem(rem(x, 2) + div(x, 2), 2), rem(rem(y, 2) + div(y, 2), 2), div(x, 2), div(y, 2)]
    hops = [device(x_at[0], y, z, core), device(x, y_at[0], z, core), device(x_at[1], y, z, core), device(x, y_at[1], z, core)]
    across = [
        device(x_at[0], y_at[0], z, core),
        device(x_at[1], y_at[0], z, core),
        device(x_at[1], y_at[1], z, core),
        device(x_at[0], y_at[1], z, core),
    ]

    def trio(d):
        return [(across[d], 1, 1), (hops[d], 1, 0), (hops[(d + 1) % 4], 0, 1)]

    own_cols = pl.ds(pl.multiple_of(core * 512, 512), 512)
    other_cols = pl.ds(pl.multiple_of(other * 512, 512), 512)
    loads = [
        pltpu.make_async_copy(act, act_v.at[0], load_sem.at[0]),
        pltpu.make_async_copy(og.at[:, own_cols], og_v.at[0], load_sem.at[1]),
        pltpu.make_async_copy(old.at[core], old_v.at[core, 0], load_sem.at[2]),
        pltpu.make_async_copy(old.at[core + 2], old_v.at[core, 1], load_sem.at[3]),
    ]
    for load in loads:
        load.start()

    barrier = pltpu.get_barrier_semaphore()
    for near in [partner, *hops, *across, along(1), along(-1)]:
        pl.semaphore_signal(barrier, inc=1, device_id=near, device_id_type=MESH)
    pl.semaphore_wait(barrier, 11)

    def spread(k):
        for far in (along(1 << k), along(-(1 << k))):
            pl.semaphore_signal(know.at[k], inc=1, device_id=far, device_id_type=MESH)

    swaps = []
    for t in range(2):
        half_rows = slice(256 * t, 256 * t + 256)
        swaps += [
            copy_to(og.at[half_rows, other_cols], og_v.at[1, half_rows], core_send.at[2 * t], core_recv.at[2 * t], partner),
            copy_to(act.at[half_rows], act_v.at[1, half_rows], core_send.at[2 * t + 1], core_recv.at[2 * t + 1], partner),
        ]
    swaps += [
        copy_to(old.at[other], old_v.at[core, 0], core_send.at[4], core_recv.at[4], partner),
        copy_to(old.at[other + 2], old_v.at[core, 1], core_send.at[5], core_recv.at[5], partner),
    ]
    for swap in swaps:
        swap.start()
    spread(0)

    def local_term(side, first, count, add):
        for m in range(4):
            rows = slice(128 * m, 128 * m + 128)
            grad_t[rows, first : first + count] = og_v[side, first : first + count, rows].T
        term = dot(grad_t[:, first : first + count], act_v[side, first : first + count])
        for q in range(4):
            value = term[:, q * 128 : (q + 1) * 128]
            acc[q] = acc[q] + value if add else value

    for load in loads:
        load.wait()
    local_term(0, 0, 512, False)
    pl.semaphore_wait(know.at[0], 2)
    spread(1)
    for t in range(2):
        swaps[2 * t].wait_recv()
        swaps[2 * t + 1].wait_recv()
        local_term(1, 256 * t, 256, True)

    got = [got0, got1]
    base = [jnp.int32(0)] * 4
    sums = []

    def send_sum(k, q):
        size = 128 >> (2 * k)
        d = (q + 2 * k) % 4
        first, second = bits[d], bits[(d + 1) % 4]
        for e, (to, a, b) in enumerate(trio(d)):
            j = (first + a - 2 * a * first) * 2 + (second + b - 2 * b * second)
            away = pl.multiple_of(base[q] + size * j, size)
            copy = copy_to(
                acc.at[q, pl.ds(away, size)], got[k].at[q, e], sum_send.at[k, q, e], sum_recv.at[k, q, e], to
            )
            copy.start()
            sums.append(copy)
        base[q] = base[q] + size * (first * 2 + second)

    def take_sum(k, q):
        size = 128 >> (2 * k)
        keep = pl.ds(pl.multiple_of(base[q], size), size)
        for e in range(3):
            sums[k * 12 + q * 3 + e].wait_recv()
        return (acc[q, keep, :] + got[k][q, 0]) + (got[k][q, 1] + got[k][q, 2]), keep

    for q in range(4):
        send_sum(0, q)
    pl.semaphore_wait(know.at[1], 2)
    spread(2)
    swaps[4].wait_recv()
    swaps[5].wait_recv()

    slice_cols = pl.ds(pl.multiple_of((bits[2] * 2 + bits[3]) * 128, 128), 128)
    mine = old_v.at[bits[1], bits[0], :, slice_cols]
    half = div(z_lo, 8)
    stage = pltpu.make_async_copy(mine, column.at[pos, half], near_sem.at[0])
    stage.start()
    pl.semaphore_wait(know.at[2], 2)
    spread(3)
    columns = []
    for i, k in enumerate([8, -7, 7, -6, 6, -5, 5, -4, 4, -3, 3, -2, 2, -1, 1]):
        copy = copy_to(mine, column.at[pos, half], col_send.at[i], col_recv.at[i], along(k))
        copy.start()
        columns.append(copy)
    for q in range(4):
        value, keep = take_sum(0, q)
        acc[q, keep, :] = value
        send_sum(1, q)
    stage.wait()
    for q in range(4):
        value, keep = take_sum(1, q)
        for h in range(2):
            shard[2 * q + h] = value[16 * h : 16 * h + 16]

    around = [-4, 3, -3, 2, -2, 1, -1]
    to_parts = []
    for i, k in enumerate(around):
        copy = copy_to(
            shard.at[rem(pos + (k + 8), 8)], parts.at[i], part_send.at[i], part_recv.at[i], along(k)
        )
        copy.start()
        to_parts.append(copy)

    for copy in columns:
        copy.wait_recv()

    number = bits[0] + 2 * bits[1] + 4 * bits[2] + 8 * bits[3]
    slots = [div(number, 1 << r) + rem(number, 1 << r) * (1 << (4 - r)) for r in range(4)]
    stages = [
        pltpu.make_async_copy(column.at[pl.ds(2 * r, 2)], planes.at[r, slots[r]], near_sem.at[1 + r])
        for r in range(4)
    ]
    for copy in stages:
        copy.start()
    for copy in stages:
        copy.wait()
    spreads = []

    def send_plane(k):
        for r in range(4):
            size = 1 << (2 * k)
            first = pl.ds(slots[r] - rem(slots[r], size), size)
            for e, (to, _, _) in enumerate(trio((r + 2 * k) % 4)):
                copy = copy_to(
                    planes.at[r, first], planes.at[r, first], plane_send.at[k, r, e], plane_recv.at[k, r, e], to
                )
                copy.start()
                spreads.append(copy)

    def take_plane(k):
        for copy in spreads[12 * k : 12 * k + 12]:
            copy.wait_recv()

    send_plane(0)

    total = shard[pos]
    for i in range(7):
        to_parts[i].wait_recv()
        total = total + parts[i]
    blocks[blk] = total
    pl.semaphore_wait(know.at[3], 2)
    to_blocks = []
    for k in range(1, 4):
        copy = copy_to(
            blocks.at[blk], blocks.at[blk], block_send.at[k - 1], block_recv.at[k - 1], along(8 * k)
        )
        copy.start()
        to_blocks.append(copy)

    take_plane(0)
    send_plane(1)

    for copy in to_blocks:
        copy.wait_recv()
    pieces[pos] = (((blocks[0] + blocks[1]) + blocks[2]) + blocks[3]).astype(BF16)
    to_pieces = []
    for i, k in enumerate(around):
        copy = copy_to(pieces.at[pos], pieces.at[pos], piece_send.at[i], piece_recv.at[i], along(k))
        copy.start()
        to_pieces.append(copy)
    for copy in to_pieces:
        copy.wait_recv()

    for q in range(4):
        for h in range(2):
            first = pl.multiple_of(base[q] + 16 * h, 16)
            grad[pl.ds(first, 16), q * 128 : (q + 1) * 128] = pieces[2 * q + h]
    gathers = []

    def send_grad(k):
        size = 128 >> (2 * k)
        for q in range(4):
            d = (q + 2 * k) % 4
            part = grad.at[pl.ds(pl.multiple_of(base[q], size), size), q * 128 : (q + 1) * 128]
            for e, (to, _, _) in enumerate(trio(d)):
                copy = copy_to(part, part, grad_send.at[k, q, e], grad_recv.at[k, q, e], to)
                copy.start()
                gathers.append(copy)
            base[q] = base[q] - size * (bits[d] * 2 + bits[(d + 1) % 4])

    send_grad(1)
    take_plane(1)
    for r in range(4):

        def lay(slot, carry):
            bit = [rem(div(slot, 1 << ((d - r) % 4)), 2) for d in range(4)]
            quarter = bit[2] * 2 + bit[3]
            for b in range(2):
                for a in range(2):
                    first = pl.multiple_of((a * 8 + 2 * r + b) * 32 + bit[1] * 16, 16)
                    old_full[bit[0], quarter, pl.ds(first, 16), :] = planes[r, slot, b, a]
            return carry

        lax.fori_loop(0, 16, lay, 0)

    for copy in gathers:
        copy.wait_recv()
    send_grad(0)
    for copy in gathers[12:]:
        copy.wait_recv()

    def eye_of(m):
        row = lax.broadcasted_iota(jnp.int32, (128, 512), 0) + m * 128
        return (row == lax.broadcasted_iota(jnp.int32, (128, 512), 1)).astype(F32)

    def flip(m, carry):
        rows = pl.ds(pl.multiple_of(m * 128, 128), 128)
        grad_t[rows, :] = grad[:, rows].T
        return carry

    lax.fori_loop(0, 4, flip, 0, unroll=True)

    def gram(m, carry):
        rows = pl.ds(pl.multiple_of(m * 128, 128), 128)
        eye = eye_of(m)
        sums_now = []
        for chain in range(2):
            left, right = (grad_t, grad) if chain == 0 else (grad, grad_t)
            term = dot(left[rows, :], right[...])
            quarters = [old_full[chain, q, rows, :] for q in range(4)]
            value = jnp.concatenate(quarters, axis=1) + term
            new_full[chain, rows, :] = value
            damped = value + DAMPING * eye
            sums_now.append(carry[chain] + jnp.sum(damped * damped, axis=0, keepdims=True))
        return tuple(sums_now)

    zero = jnp.zeros((1, 512), F32)
    squares = lax.fori_loop(0, 4, gram, (zero, zero), unroll=True)
    own_first = pl.multiple_of(z_lo * 32 + 16 * core, 16)
    other_first = pl.multiple_of(z_lo * 32 + 16 * other, 16)
    outs, sends = [], []
    for chain in range(2):
        outs.append(
            pltpu.make_async_copy(
                new_full.at[chain, pl.ds(own_first, 16)], stats.at[2 * chain + core], out_sem.at[chain]
            )
        )
        sends.append(
            copy_to(
                new_full.at[chain, pl.ds(other_first, 16)], stats.at[2 * chain + core],
                out_send.at[chain], out_recv.at[chain], partner,
            )
        )
        outs[-1].start()
        sends[-1].start()

    scales = [2.5 / jnp.sqrt(jnp.sum(part, axis=1, keepdims=True)) for part in squares]
    quarters = [jnp.sqrt(jnp.sqrt(scale)) for scale in scales]

    def begin(m, carry):
        rows = pl.ds(pl.multiple_of(m * 128, 128), 128)
        eye = eye_of(m)
        for chain in range(2):
            iterate = scales[chain] * (new_full[chain, rows, :] + DAMPING * eye)
            factor0[chain, rows, :] = ((5.0 * eye - iterate) * 0.25).astype(BF16)
            high = iterate.astype(BF16)
            split[chain, 0, rows, :] = high
            split[chain, 1, rows, :] = (iterate - high.astype(F32)).astype(BF16)
        return carry

    lax.fori_loop(0, 4, begin, 0, unroll=True)

    def multiply(step, carry):
        for chain in range(2):
            whole = factor0[chain]
            iterate = dot(split[chain, 0], whole) + dot(split[chain, 1], whole)
            high = iterate.astype(BF16)
            split[chain, 0] = high
            split[chain, 1] = (iterate - high.astype(F32)).astype(BF16)
        return carry

    lax.fori_loop(0, 3, multiply, 0)

    row_ids = lax.broadcasted_iota(jnp.int32, (256, 512), 0)
    column_ids = lax.broadcasted_iota(jnp.int32, (256, 512), 1)
    for top in range(2):
        rows = slice(256 * top, 256 * top + 256)
        eye = (row_ids + 256 * top == column_ids).astype(F32)
        for chain in range(2):
            whole = factor0[chain]
            iterate = dot(split[chain, 0, rows, :], whole) + dot(split[chain, 1, rows, :], whole)
            factor1[chain, rows, :] = ((5.0 * eye - iterate) * 0.25).astype(BF16)

    chip_rows = pl.ds(pl.multiple_of(z_lo * 32, 32), 32)
    right_root = (quarters[1] * dot(factor0[1, chip_rows, :], factor1[1])).astype(BF16)
    for top in range(2):
        rows = slice(256 * top, 256 * top + 256)
        root[rows, :] = (quarters[0] * dot(factor0[0, rows, :], factor1[0])).astype(BF16)
    inner = dot(right_root, grad[...])
    high = inner.astype(BF16)
    rest = inner - high.astype(F32)
    middle = rest.astype(BF16)
    low = (rest - middle.astype(F32)).astype(BF16)
    left_root = root[...]
    total = (dot(low, left_root) + dot(middle, left_root)) + dot(high, left_root)
    upd[...] = total * math.sqrt(512)
    outs.append(
        pltpu.make_async_copy(
            upd.at[pl.ds(pl.multiple_of(16 * core, 16), 16)], update.at[core], out_sem.at[2]
        )
    )
    sends.append(
        copy_to(
            upd.at[pl.ds(pl.multiple_of(16 * other, 16), 16)], update.at[core],
            out_send.at[2], out_recv.at[2], partner,
        )
    )
    outs[-1].start()
    sends[-1].start()

    for copy in outs:
        copy.wait()
    for copy in [*swaps, *sums, *to_parts, *columns, *spreads, *to_blocks, *to_pieces, *gathers, *sends]:
        copy.wait_send()
    for copy in sends:
        copy.wait_recv()


def on_device(activations, out_grads, stats_old):
    dma = pltpu.SemaphoreType.DMA
    vmem = pltpu.VMEM
    anywhere = pl.BlockSpec(memory_space=pl.ANY)
    return pl.pallas_call(
        kernel,
        out_shape=(
            pltpu.VMEM((4, 16, 512), F32),
            pltpu.VMEM((2, 16, 512), F32),
        ),
        in_specs=[anywhere] * 3,
        out_specs=(pl.BlockSpec(memory_space=pltpu.VMEM),) * 2,
        scratch_shapes=[
            vmem((2, 512, 512), BF16),
            vmem((2, 512, 512), BF16),
            vmem((2, 2, 16, 512), F32),
            vmem((4, 512, 128), F32),
            vmem((4, 3, 128, 128), F32),
            vmem((4, 3, 32, 128), F32),
            vmem((8, 16, 128), F32),
            vmem((7, 16, 128), F32),
            vmem((4, 16, 128), F32),
            vmem((8, 16, 128), BF16),
            vmem((512, 512), BF16),
            vmem((512, 512), BF16),
            vmem((8, 2, 16, 128), F32),
            vmem((4, 16, 2, 2, 16, 128), F32),
            vmem((2, 4, 512, 128), F32),
            vmem((2, 512, 512), F32),
            vmem((2, 512, 512), BF16),
            vmem((2, 512, 512), BF16),
            vmem((2, 2, 512, 512), BF16),
            vmem((512, 512), BF16),
            vmem((32, 512), F32),
            dma((4,)),
            dma((6,)), dma((6,)),
            dma((2, 4, 3)), dma((2, 4, 3)),
            dma((7,)), dma((7,)),
            dma((3,)), dma((3,)),
            dma((7,)), dma((7,)),
            dma((2, 4, 3)), dma((2, 4, 3)),
            dma((5,)),
            dma((15,)), dma((15,)),
            dma((2, 4, 3)), dma((2, 4, 3)),
            dma((3,)),
            dma((3,)), dma((3,)),
            pltpu.SemaphoreType.REGULAR((4,)),
        ],
        compiler_params=pltpu.CompilerParams(
            collective_id=0, has_side_effects=True, vmem_limit_bytes=56 * 1024 * 1024
        ),
    )(activations, out_grads, stats_old)


def solution(mesh):
    in_specs = (P(("rep", "grp"), None), P(("rep", "grp"), None), P(None, "grp", None))
    out_specs = (P(None, "grp", None), P(None, "grp", None))
    return jax.shard_map(
        on_device, mesh=mesh, in_specs=in_specs, out_specs=out_specs, check_vma=False
    )
```

```python
import functools
import math

import jax
import jax.numpy as jnp
from jax import lax
from jax.experimental import pallas as pl
from jax.experimental.pallas import tpu as pltpu
from jax.sharding import PartitionSpec as P

MESH = pl.DeviceIdType.MESH
F32 = jnp.float32
BF16 = jnp.bfloat16
DAMPING = 0.01
ITERS = 2


SWAP, OLD, SUM, MID, PART, BLOCK, PIECE, NEAR_GRAD, GRAD, COLUMN, NEAR_PLANE, PLANE, OUT = (
    0, 2, 3, 7, 8, 9, 10, 11, 14, 15, 16, 19, 20
)


def wait_bytes(ref, sem):
    pltpu.make_async_copy(ref, ref, sem).wait()


def div(a, b):
    return lax.div(a, jnp.int32(b))


def rem(a, b):
    return lax.rem(a, jnp.int32(b))


def dot(a, b):
    return jnp.dot(a, b, preferred_element_type=F32)


def transposed_dot(a, b):
    return lax.dot_general(a, b, (((0,), (0,)), ((), ())), preferred_element_type=F32)


def copy_to(src, dst, send, recv, device):
    return pltpu.make_async_remote_copy(
        src_ref=src, dst_ref=dst, send_sem=send, recv_sem=recv, device_id=device, device_id_type=MESH
    )


def kernel(
    act, og, old, stats, update,
    act_v, og_v, old_v, acc, got0, got1, shard, parts, blocks, pieces, grad, grad_t,
    column, planes, old_full, new_full, factor0, factor1, split, root, upd,
    here, sent, come, know,
):
    rep, grp = lax.axis_index("rep"), lax.axis_index("grp")
    z_hi, xy = rem(rep, 2), div(rep, 2)
    y, x = rem(xy, 4), div(xy, 4)
    core, z_lo = rem(grp, 2), div(grp, 2)
    z = z_hi * 16 + z_lo
    blk, pos = div(z, 8), rem(z, 8)
    other = 1 - core

    def device(x_at, y_at, z_at, core_at):
        return {"rep": (x_at * 4 + y_at) * 2 + div(z_at, 16), "grp": rem(z_at, 16) * 2 + core_at}

    def along(k):
        return device(x, y, rem(z + (k + 32), 32), core)

    partner = device(x, y, z, other)
    x_at = [x + 1 - 2 * rem(x, 2), 3 - x]
    y_at = [y + 1 - 2 * rem(y, 2), 3 - y]
    bits = [rem(rem(x, 2) + div(x, 2), 2), rem(rem(y, 2) + div(y, 2), 2), div(x, 2), div(y, 2)]
    hops = [device(x_at[0], y, z, core), device(x, y_at[0], z, core), device(x_at[1], y, z, core), device(x, y_at[1], z, core)]
    across = [
        device(x_at[0], y_at[0], z, core),
        device(x_at[1], y_at[0], z, core),
        device(x_at[1], y_at[1], z, core),
        device(x_at[0], y_at[1], z, core),
    ]

    def chip_of(d, e):
        return (across[d], hops[d], hops[(d + 1) % 4])[e]

    def number_of(d, e):
        first, second = bits[d], bits[(d + 1) % 4]
        if e in (0, 1):
            first = 1 - first
        if e in (0, 2):
            second = 1 - second
        return first * 2 + second

    barrier = pltpu.get_barrier_semaphore()
    for near in [partner, *hops, *across, along(1), along(-1)]:
        pl.semaphore_signal(barrier, inc=1, device_id=near, device_id_type=MESH)

    own_cols = pl.ds(pl.multiple_of(core * 512, 512), 512)
    other_cols = pl.ds(pl.multiple_of(other * 512, 512), 512)
    loads = [
        pltpu.make_async_copy(act, act_v.at[0], here.at[0]),
        pltpu.make_async_copy(og.at[:, own_cols], og_v.at[0], here.at[0]),
        pltpu.make_async_copy(old.at[core], old_v.at[core, 0], here.at[1]),
        pltpu.make_async_copy(old.at[core + 2], old_v.at[core, 1], here.at[1]),
    ]
    for load in loads:
        load.start()

    pl.semaphore_wait(barrier, 11)

    def spread(k):
        for far in (along(1 << k), along(-(1 << k))):
            pl.semaphore_signal(know.at[k], inc=1, device_id=far, device_id_type=MESH)

    swaps = []
    for t in range(2):
        half_rows = slice(256 * t, 256 * t + 256)
        pair = sent.at[SWAP + t], come.at[SWAP + t], partner
        swaps += [
            copy_to(og.at[half_rows, other_cols], og_v.at[1, half_rows], *pair),
            copy_to(act.at[half_rows], act_v.at[1, half_rows], *pair),
        ]
    pair = sent.at[OLD], come.at[OLD], partner
    swaps += [
        copy_to(old.at[other], old_v.at[core, 0], *pair),
        copy_to(old.at[other + 2], old_v.at[core, 1], *pair),
    ]
    for swap in swaps:
        swap.start()
    spread(0)

    def local_term(side, first, count, add):
        for m in range(4):
            rows = slice(128 * m, 128 * m + 128)
            grad_t[rows, first : first + count] = og_v[side, first : first + count, rows].T
        term = dot(grad_t[:, first : first + count], act_v[side, first : first + count])
        for q in range(4):
            value = term[:, q * 128 : (q + 1) * 128]
            acc[q] = acc[q] + value if add else value

    wait_bytes(og_v, here.at[0])
    local_term(0, 0, 512, False)
    for t in range(2):
        wait_bytes(og_v.at[1], come.at[SWAP + t])
        local_term(1, 256 * t, 256, True)

    def rows_at(q, e, s):
        return pl.ds(pl.multiple_of(128 * number_of(q, e) + 32 * number_of((q + 2) % 4, s), 32), 32)

    sums = {}
    for s in range(4):
        for q in range(4):
            for e in range(3):
                sums[q, e, s] = copy_to(
                    acc.at[q, rows_at(q, e, s)], got0.at[s, q, e], sent.at[SUM + s], come.at[SUM + s], chip_of(q, e)
                )
                sums[q, e, s].start()
    pl.semaphore_wait(know.at[0], 2)
    spread(1)
    wait_bytes(old_v.at[0], here.at[1])
    wait_bytes(old_v.at[0], come.at[OLD])

    slice_cols = pl.ds(pl.multiple_of((bits[2] * 2 + bits[3]) * 128, 128), 128)
    mine = old_v.at[bits[1], bits[0], :, slice_cols]
    half = div(z_lo, 8)
    stage = pltpu.make_async_copy(mine, column.at[pos, half], here.at[2])
    stage.start()
    pl.semaphore_wait(know.at[1], 2)
    spread(2)

    def take_sum(q, s):
        return (acc[q, rows_at(q, 3, s), :] + got0[s, q, 0]) + (got0[s, q, 1] + got0[s, q, 2])

    mids = {}
    columns = []
    for s in range(3):
        wait_bytes(got0.at[s], come.at[SUM + s])
        for q in range(4):
            acc[q, rows_at(q, 3, s), :] = take_sum(q, s)
            mids[q, s] = copy_to(
                acc.at[q, rows_at(q, 3, s)], got1.at[q, s], sent.at[MID], come.at[MID], chip_of((q + 2) % 4, s)
            )
            mids[q, s].start()
        if s == 0:
            stage.wait()
            pl.semaphore_wait(know.at[2], 2)
            spread(3)
            for i, k in enumerate([8, -7, 7, -6, 6, -5, 5, -4, 4, -3, 3, -2, 2, -1, 1]):
                copy = copy_to(mine, column.at[pos, half], sent.at[COLUMN], come.at[COLUMN], along(k))
                copy.start()
                columns.append(copy)
    wait_bytes(got0.at[3], come.at[SUM + 3])
    wait_bytes(got1, come.at[MID])
    for q in range(4):
        value = take_sum(q, 3)
        value = value + ((got1[q, 0] + got1[q, 1]) + got1[q, 2])
        for h in range(2):
            shard[2 * q + h] = value[16 * h : 16 * h + 16]

    around = [-4, 3, -3, 2, -2, 1, -1]
    to_parts = []
    for i, k in enumerate(around):
        copy = copy_to(
            shard.at[rem(pos + (k + 8), 8)], parts.at[i], sent.at[PART], come.at[PART], along(k)
        )
        copy.start()
        to_parts.append(copy)

    wait_bytes(old_full.at[0, 0, pl.ds(0, 240)], come.at[COLUMN])

    number = bits[0] + 2 * bits[1] + 4 * bits[2] + 8 * bits[3]
    slots = [div(number, 1 << r) + rem(number, 1 << r) * (1 << (4 - r)) for r in range(4)]
    stages = [
        pltpu.make_async_copy(column.at[pl.ds(2 * r, 2)], planes.at[r, slots[r]], here.at[3])
        for r in range(4)
    ]
    for copy in stages:
        copy.start()
    wait_bytes(planes.at[0, pl.ds(0, 4)], here.at[3])
    near_planes, far_planes = {}, {}

    def slots_at(r, e):
        flip = number_of(r, e)
        first, second = div(flip, 2), rem(flip, 2)
        return slots[r] - rem(slots[r], 4) + first + 2 * second

    def forward_plane(s):
        if s < 3:
            wait_bytes(planes.at[0, pl.ds(0, 4)], come.at[NEAR_PLANE + s])
        for r in range(4):
            at = slots_at(r, s)
            for e in range(3):
                far_planes[r, e, s] = copy_to(
                    planes.at[r, at], planes.at[r, at], sent.at[PLANE], come.at[PLANE], chip_of((r + 2) % 4, e)
                )
                far_planes[r, e, s].start()

    for r in range(4):
        for e in range(3):
            near_planes[r, e] = copy_to(
                planes.at[r, slots[r]], planes.at[r, slots[r]], sent.at[NEAR_PLANE + e], come.at[NEAR_PLANE + e], chip_of(r, e)
            )
            near_planes[r, e].start()
    forward_plane(3)

    total = shard[pos]
    for i in range(7):
        if i == 0:
            wait_bytes(parts, come.at[PART])
        total = total + parts[i]
    blocks[blk] = total
    pl.semaphore_wait(know.at[3], 2)
    to_blocks = []
    for k in range(1, 4):
        copy = copy_to(
            blocks.at[blk], blocks.at[blk], sent.at[BLOCK], come.at[BLOCK], along(8 * k)
        )
        copy.start()
        to_blocks.append(copy)

    for s in (1, 2, 0):
        forward_plane(s)

    wait_bytes(blocks.at[pl.ds(0, 3)], come.at[BLOCK])
    pieces[pos] = (((blocks[0] + blocks[1]) + blocks[2]) + blocks[3]).astype(BF16)
    to_pieces = []
    for i, k in enumerate(around):
        copy = copy_to(pieces.at[pos], pieces.at[pos], sent.at[PIECE], come.at[PIECE], along(k))
        copy.start()
        to_pieces.append(copy)
    wait_bytes(pieces.at[pl.ds(0, 7)], come.at[PIECE])

    for q in range(4):
        grad[rows_at(q, 3, 3), q * 128 : (q + 1) * 128] = jnp.concatenate([pieces[2 * q], pieces[2 * q + 1]], axis=0)
    near_grads, far_grads = {}, {}

    def forward_grad(s):
        if s < 3:
            wait_bytes(grad.at[pl.ds(0, 32)], come.at[NEAR_GRAD + s])
        for q in range(4):
            part = grad.at[rows_at(q, 3, s), q * 128 : (q + 1) * 128]
            for e in range(3):
                far_grads[q, e, s] = copy_to(
                    part, part, sent.at[GRAD], come.at[GRAD], chip_of(q, e)
                )
                far_grads[q, e, s].start()

    for q in range(4):
        part = grad.at[rows_at(q, 3, 3), q * 128 : (q + 1) * 128]
        for e in range(3):
            near_grads[q, e] = copy_to(
                part, part, sent.at[NEAR_GRAD + e], come.at[NEAR_GRAD + e], chip_of((q + 2) % 4, e)
            )
            near_grads[q, e].start()
    forward_grad(3)
    for s in (1, 2, 0):
        forward_grad(s)
    wait_bytes(planes.at[pl.ds(0, 3)], come.at[PLANE])
    for r in range(4):

        def lay(slot, carry):
            bit = [rem(div(slot, 1 << ((d - r) % 4)), 2) for d in range(4)]
            quarter = bit[2] * 2 + bit[3]
            for b in range(2):
                for a in range(2):
                    first = pl.multiple_of((a * 8 + 2 * r + b) * 32 + bit[1] * 16, 16)
                    old_full[bit[0], quarter, pl.ds(first, 16), :] = planes[r, slot, b, a]
            return carry

        lax.fori_loop(0, 16, lay, 0)

    wait_bytes(grad.at[pl.ds(0, 384)], come.at[GRAD])

    def eye_of(m):
        row = lax.broadcasted_iota(jnp.int32, (128, 512), 0) + m * 128
        return (row == lax.broadcasted_iota(jnp.int32, (128, 512), 1)).astype(F32)

    def flip(m, carry):
        rows = pl.ds(pl.multiple_of(m * 128, 128), 128)
        grad_t[rows, :] = grad[:, rows].T
        return carry

    lax.fori_loop(0, 4, flip, 0, unroll=True)

    def gram(m, carry):
        rows = pl.ds(pl.multiple_of(m * 128, 128), 128)
        eye = eye_of(m)
        sums_now = []
        for chain in range(2):
            left, right = (grad_t, grad) if chain == 0 else (grad, grad_t)
            term = dot(left[rows, :], right[...])
            quarters = [old_full[chain, q, rows, :] for q in range(4)]
            value = jnp.concatenate(quarters, axis=1) + term
            new_full[chain, rows, :] = value
            damped = value + DAMPING * eye
            sums_now.append(carry[chain] + jnp.sum(damped * damped, axis=0, keepdims=True))
        return tuple(sums_now)

    zero = jnp.zeros((1, 512), F32)
    squares = lax.fori_loop(0, 4, gram, (zero, zero), unroll=True)
    own_first = pl.multiple_of(z_lo * 32 + 16 * core, 16)
    other_first = pl.multiple_of(z_lo * 32 + 16 * other, 16)
    outs, sends = [], []
    for chain in range(2):
        outs.append(
            pltpu.make_async_copy(
                new_full.at[chain, pl.ds(own_first, 16)], stats.at[2 * chain + core], here.at[4]
            )
        )
        sends.append(
            copy_to(
                new_full.at[chain, pl.ds(other_first, 16)], stats.at[2 * chain + core],
                sent.at[OUT], come.at[OUT], partner,
            )
        )
        outs[-1].start()
        sends[-1].start()

    scales = [2.5 / jnp.sqrt(jnp.sum(part, axis=1, keepdims=True)) for part in squares]
    quarters = [jnp.sqrt(jnp.sqrt(scale)) for scale in scales]

    def begin(m, carry):
        rows = pl.ds(pl.multiple_of(m * 128, 128), 128)
        eye = eye_of(m)
        for chain in range(2):
            iterate = scales[chain] * (new_full[chain, rows, :] + DAMPING * eye)
            factor = ((5.0 * eye - iterate) * 0.25).astype(BF16)
            factor0[chain, rows, :] = factor
            factor0[chain, pl.ds(pl.multiple_of(m * 128 + 512, 128), 128), :] = factor
            high = iterate.astype(BF16)
            split[chain, rows, :512] = high
            split[chain, rows, 512:] = (iterate - high.astype(F32)).astype(BF16)
        return carry

    lax.fori_loop(0, 4, begin, 0, unroll=True)

    def multiply(step, carry):
        for chain in range(2):
            iterate = dot(split[chain], factor0[chain])
            high = iterate.astype(BF16)
            split[chain, :, :512] = high
            split[chain, :, 512:] = (iterate - high.astype(F32)).astype(BF16)
        return carry

    lax.fori_loop(0, 3, multiply, 0)

    row_ids = lax.broadcasted_iota(jnp.int32, (256, 512), 0)
    column_ids = lax.broadcasted_iota(jnp.int32, (256, 512), 1)
    for top in range(2):
        rows = slice(256 * top, 256 * top + 256)
        eye = (row_ids + 256 * top == column_ids).astype(F32)
        for chain in range(2):
            iterate = dot(split[chain, rows, :], factor0[chain])
            factor1[chain, rows, :] = ((5.0 * eye - iterate) * 0.25).astype(BF16)

    chip_rows = pl.ds(pl.multiple_of(z_lo * 32, 32), 32)
    right_root = (quarters[1] * dot(factor0[1, chip_rows, :], factor1[1])).astype(BF16)
    for top in range(2):
        rows = slice(256 * top, 256 * top + 256)
        root[rows, :] = (quarters[0] * dot(factor0[0, rows, :], factor1[0])).astype(BF16)
    inner = dot(right_root, grad[...])
    high = inner.astype(BF16)
    rest = inner - high.astype(F32)
    middle = rest.astype(BF16)
    low = (rest - middle.astype(F32)).astype(BF16)
    total = dot(jnp.concatenate([low, middle, high], axis=0), root[...])
    total = (total[:32] + total[32:64]) + total[64:]
    upd[...] = total * math.sqrt(512)
    outs.append(
        pltpu.make_async_copy(
            upd.at[pl.ds(pl.multiple_of(16 * core, 16), 16)], update.at[core], here.at[4]
        )
    )
    sends.append(
        copy_to(
            upd.at[pl.ds(pl.multiple_of(16 * other, 16), 16)], update.at[core],
            sent.at[OUT], come.at[OUT], partner,
        )
    )
    outs[-1].start()
    sends[-1].start()

    wait_bytes(new_full.at[0, pl.ds(0, 48)], here.at[4])
    for sems in (come, sent):
        wait_bytes(new_full.at[0, pl.ds(0, 48)], sems.at[OUT])
    for t in range(2):
        wait_bytes(og_v.at[1], sent.at[SWAP + t])
    wait_bytes(old_v.at[0], sent.at[OLD])
    for s in range(4):
        wait_bytes(got0.at[s], sent.at[SUM + s])
    wait_bytes(got1, sent.at[MID])
    wait_bytes(parts, sent.at[PART])
    wait_bytes(blocks.at[pl.ds(0, 3)], sent.at[BLOCK])
    wait_bytes(pieces.at[pl.ds(0, 7)], sent.at[PIECE])
    for e in range(3):
        wait_bytes(grad.at[pl.ds(0, 32)], sent.at[NEAR_GRAD + e])
        wait_bytes(planes.at[0, pl.ds(0, 4)], sent.at[NEAR_PLANE + e])
    wait_bytes(grad.at[pl.ds(0, 384)], sent.at[GRAD])
    wait_bytes(old_full.at[0, 0, pl.ds(0, 240)], sent.at[COLUMN])
    wait_bytes(planes.at[pl.ds(0, 3)], sent.at[PLANE])


def on_device(activations, out_grads, stats_old):
    dma = pltpu.SemaphoreType.DMA
    vmem = pltpu.VMEM
    anywhere = pl.BlockSpec(memory_space=pl.ANY)
    return pl.pallas_call(
        kernel,
        out_shape=(
            pltpu.VMEM((4, 16, 512), F32),
            pltpu.VMEM((2, 16, 512), F32),
        ),
        in_specs=[anywhere] * 3,
        out_specs=(pl.BlockSpec(memory_space=pltpu.VMEM),) * 2,
        scratch_shapes=[
            vmem((2, 512, 512), BF16),
            vmem((2, 512, 512), BF16),
            vmem((2, 2, 16, 512), F32),
            vmem((4, 512, 128), F32),
            vmem((4, 4, 3, 32, 128), F32),
            vmem((4, 3, 32, 128), F32),
            vmem((8, 16, 128), F32),
            vmem((7, 16, 128), F32),
            vmem((4, 16, 128), F32),
            vmem((8, 16, 128), BF16),
            vmem((512, 512), BF16),
            vmem((512, 512), BF16),
            vmem((8, 2, 16, 128), F32),
            vmem((4, 16, 2, 2, 16, 128), F32),
            vmem((2, 4, 512, 128), F32),
            vmem((2, 512, 512), F32),
            vmem((2, 1024, 512), BF16),
            vmem((2, 512, 512), BF16),
            vmem((2, 512, 1024), BF16),
            vmem((512, 512), BF16),
            vmem((32, 512), F32),
            dma((5,)),
            dma((21,)),
            dma((21,)),
            pltpu.SemaphoreType.REGULAR((4,)),
        ],
        compiler_params=pltpu.CompilerParams(
            collective_id=0, has_side_effects=True, vmem_limit_bytes=56 * 1024 * 1024
        ),
    )(activations, out_grads, stats_old)


def solution(mesh):
    in_specs = (P(("rep", "grp"), None), P(("rep", "grp"), None), P(None, "grp", None))
    out_specs = (P(None, "grp", None), P(None, "grp", None))
    return jax.shard_map(
        on_device, mesh=mesh, in_specs=in_specs, out_specs=out_specs, check_vma=False
    )
```

```python
import functools
import math

import jax
import jax.numpy as jnp
from jax import lax
from jax.experimental import pallas as pl
from jax.experimental.pallas import tpu as pltpu
from jax.sharding import PartitionSpec as P

MESH = pl.DeviceIdType.MESH
F32 = jnp.float32
BF16 = jnp.bfloat16
DAMPING = 0.01
ITERS = 2


SWAP, OLD, SUM, MID, PART, BLOCK, PIECE, NEAR_GRAD, GRAD, COLUMN, NEAR_PLANE, PLANE, OUT = (
    0, 2, 3, 7, 8, 9, 10, 11, 14, 15, 16, 19, 20
)


def wait_bytes(ref, sem):
    pltpu.make_async_copy(ref, ref, sem).wait()


def div(a, b):
    return lax.div(a, jnp.int32(b))


def rem(a, b):
    return lax.rem(a, jnp.int32(b))


def dot(a, b):
    return jnp.dot(a, b, preferred_element_type=F32)


def transposed_dot(a, b):
    return lax.dot_general(a, b, (((0,), (0,)), ((), ())), preferred_element_type=F32)


def copy_to(src, dst, send, recv, device):
    return pltpu.make_async_remote_copy(
        src_ref=src, dst_ref=dst, send_sem=send, recv_sem=recv, device_id=device, device_id_type=MESH
    )


def kernel(
    act, og, old, stats, update,
    act_v, og_v, old_v, acc, got0, got1, shard, parts, blocks, pieces, grad, grad_t,
    column, planes, old_full, new_full, factor0, factor1, left, square, right, root, upd,
    here, sent, come, know,
):
    rep, grp = lax.axis_index("rep"), lax.axis_index("grp")
    z_hi, xy = rem(rep, 2), div(rep, 2)
    y, x = rem(xy, 4), div(xy, 4)
    core, z_lo = rem(grp, 2), div(grp, 2)
    z = z_hi * 16 + z_lo
    blk, pos = div(z, 8), rem(z, 8)
    other = 1 - core
    tile = rem(core + (x + y + z), 2)
    other_tile = 1 - tile

    def device(x_at, y_at, z_at, tile_at):
        core_at = rem(tile_at + (x_at + y_at + z_at), 2)
        return {"rep": (x_at * 4 + y_at) * 2 + div(z_at, 16), "grp": rem(z_at, 16) * 2 + core_at}

    def along(k):
        return device(x, y, rem(z + (k + 32), 32), tile)

    partner = device(x, y, z, other_tile)
    x_at = [x + 1 - 2 * rem(x, 2), 3 - x]
    y_at = [y + 1 - 2 * rem(y, 2), 3 - y]
    bits = [rem(rem(x, 2) + div(x, 2), 2), rem(rem(y, 2) + div(y, 2), 2), div(x, 2), div(y, 2)]
    hops = [device(x_at[0], y, z, tile), device(x, y_at[0], z, tile), device(x_at[1], y, z, tile), device(x, y_at[1], z, tile)]
    across = [
        device(x_at[0], y_at[0], z, tile),
        device(x_at[1], y_at[0], z, tile),
        device(x_at[1], y_at[1], z, tile),
        device(x_at[0], y_at[1], z, tile),
    ]

    def chip_of(d, e):
        return (across[d], hops[d], hops[(d + 1) % 4])[e]

    def number_of(d, e):
        first, second = bits[d], bits[(d + 1) % 4]
        if e in (0, 1):
            first = 1 - first
        if e in (0, 2):
            second = 1 - second
        return first * 2 + second

    barrier = pltpu.get_barrier_semaphore()
    for near in [partner, *hops, *across, along(1), along(-1)]:
        pl.semaphore_signal(barrier, inc=1, device_id=near, device_id_type=MESH)

    own_cols = pl.ds(pl.multiple_of(tile * 512, 512), 512)
    other_cols = pl.ds(pl.multiple_of(other_tile * 512, 512), 512)
    loads = [
        pltpu.make_async_copy(act, act_v.at[0], here.at[0]),
        pltpu.make_async_copy(og.at[:, own_cols], og_v.at[0], here.at[0]),
        pltpu.make_async_copy(old.at[tile], old_v.at[core, 0], here.at[1]),
        pltpu.make_async_copy(old.at[tile + 2], old_v.at[core, 1], here.at[1]),
    ]
    for load in loads:
        load.start()

    pl.semaphore_wait(barrier, 11)

    def spread(k):
        for far in (along(1 << k), along(-(1 << k))):
            pl.semaphore_signal(know.at[k], inc=1, device_id=far, device_id_type=MESH)

    swaps = []
    for t in range(2):
        half_rows = slice(256 * t, 256 * t + 256)
        pair = sent.at[SWAP + t], come.at[SWAP + t], partner
        swaps += [
            copy_to(og.at[half_rows, other_cols], og_v.at[1, half_rows], *pair),
            copy_to(act.at[half_rows], act_v.at[1, half_rows], *pair),
        ]
    pair = sent.at[OLD], come.at[OLD], partner
    swaps += [
        copy_to(old.at[other_tile], old_v.at[core, 0], *pair),
        copy_to(old.at[other_tile + 2], old_v.at[core, 1], *pair),
    ]
    for swap in swaps:
        swap.start()
    spread(0)

    def local_term(side, first, count, add):
        for m in range(4):
            rows = slice(128 * m, 128 * m + 128)
            grad_t[rows, first : first + count] = og_v[side, first : first + count, rows].T
        term = dot(grad_t[:, first : first + count], act_v[side, first : first + count])
        for q in range(4):
            value = term[:, q * 128 : (q + 1) * 128]
            acc[q] = acc[q] + value if add else value

    wait_bytes(og_v, here.at[0])
    local_term(0, 0, 512, False)
    pl.semaphore_wait(know.at[0], 2)
    spread(1)
    for t in range(2):
        wait_bytes(og_v.at[1], come.at[SWAP + t])
        local_term(1, 256 * t, 256, True)

    def rows_at(q, e, s):
        return pl.ds(pl.multiple_of(128 * number_of(q, e) + 32 * number_of((q + 2) % 4, s), 32), 32)

    sums = {}
    for s in range(4):
        for q in range(4):
            for e in range(3):
                sums[q, e, s] = copy_to(
                    acc.at[q, rows_at(q, e, s)], got0.at[s, q, e], sent.at[SUM + s], come.at[SUM + s], chip_of(q, e)
                )
                sums[q, e, s].start()
    wait_bytes(old_v.at[0], here.at[1])
    wait_bytes(old_v.at[0], come.at[OLD])

    slice_cols = pl.ds(pl.multiple_of((bits[2] * 2 + bits[3]) * 128, 128), 128)
    mine = old_v.at[bits[1], bits[0], :, slice_cols]
    half = div(z_lo, 8)
    stage = pltpu.make_async_copy(mine, column.at[pos, half], here.at[2])
    stage.start()
    pl.semaphore_wait(know.at[1], 2)
    spread(2)

    def take_sum(q, s):
        return (acc[q, rows_at(q, 3, s), :] + got0[s, q, 0]) + (got0[s, q, 1] + got0[s, q, 2])

    mids = {}
    columns = []
    for s in range(3):
        wait_bytes(got0.at[s], come.at[SUM + s])
        for q in range(4):
            acc[q, rows_at(q, 3, s), :] = take_sum(q, s)
            mids[q, s] = copy_to(
                acc.at[q, rows_at(q, 3, s)], got1.at[q, s], sent.at[MID], come.at[MID], chip_of((q + 2) % 4, s)
            )
            mids[q, s].start()
        if s == 0:
            stage.wait()
            pl.semaphore_wait(know.at[2], 2)
            spread(3)
            for i, k in enumerate([8, -7, 7, -6, 6, -5, 5, -4, 4, -3, 3, -2, 2, -1, 1]):
                copy = copy_to(mine, column.at[pos, half], sent.at[COLUMN], come.at[COLUMN], along(k))
                copy.start()
                columns.append(copy)
    wait_bytes(got0.at[3], come.at[SUM + 3])
    wait_bytes(got1, come.at[MID])
    for q in range(4):
        value = take_sum(q, 3)
        value = value + ((got1[q, 0] + got1[q, 1]) + got1[q, 2])
        for h in range(2):
            shard[2 * q + h] = value[16 * h : 16 * h + 16]

    around = [-4, 3, -3, 2, -2, 1, -1]
    to_parts = []
    for i, k in enumerate(around):
        copy = copy_to(
            shard.at[rem(pos + (k + 8), 8)], parts.at[i], sent.at[PART], come.at[PART], along(k)
        )
        copy.start()
        to_parts.append(copy)

    wait_bytes(old_full.at[0, 0, pl.ds(0, 240)], come.at[COLUMN])

    number = bits[0] + 2 * bits[1] + 4 * bits[2] + 8 * bits[3]
    slots = [div(number, 1 << r) + rem(number, 1 << r) * (1 << (4 - r)) for r in range(4)]
    stages = [
        pltpu.make_async_copy(column.at[pl.ds(2 * r, 2)], planes.at[r, slots[r]], here.at[3])
        for r in range(4)
    ]
    for copy in stages:
        copy.start()
    wait_bytes(planes.at[0, pl.ds(0, 4)], here.at[3])
    near_planes, far_planes = {}, {}

    def slots_at(r, e):
        flip = number_of(r, e)
        first, second = div(flip, 2), rem(flip, 2)
        return slots[r] - rem(slots[r], 4) + first + 2 * second

    def forward_plane(s):
        if s < 3:
            wait_bytes(planes.at[0, pl.ds(0, 4)], come.at[NEAR_PLANE + s])
        for r in range(4):
            at = slots_at(r, s)
            for e in range(3):
                far_planes[r, e, s] = copy_to(
                    planes.at[r, at], planes.at[r, at], sent.at[PLANE], come.at[PLANE], chip_of((r + 2) % 4, e)
                )
                far_planes[r, e, s].start()

    for r in range(4):
        for e in range(3):
            near_planes[r, e] = copy_to(
                planes.at[r, slots[r]], planes.at[r, slots[r]], sent.at[NEAR_PLANE + e], come.at[NEAR_PLANE + e], chip_of(r, e)
            )
            near_planes[r, e].start()
    forward_plane(3)

    total = shard[pos]
    for i in range(7):
        if i == 0:
            wait_bytes(parts, come.at[PART])
        total = total + parts[i]
    blocks[blk] = total
    pl.semaphore_wait(know.at[3], 2)
    to_blocks = []
    for k in range(1, 4):
        copy = copy_to(
            blocks.at[blk], blocks.at[blk], sent.at[BLOCK], come.at[BLOCK], along(8 * k)
        )
        copy.start()
        to_blocks.append(copy)

    for s in (1, 2, 0):
        forward_plane(s)

    wait_bytes(blocks.at[pl.ds(0, 3)], come.at[BLOCK])
    pieces[pos] = (((blocks[0] + blocks[1]) + blocks[2]) + blocks[3]).astype(BF16)
    to_pieces = []
    for i, k in enumerate(around):
        copy = copy_to(pieces.at[pos], pieces.at[pos], sent.at[PIECE], come.at[PIECE], along(k))
        copy.start()
        to_pieces.append(copy)
    wait_bytes(pieces.at[pl.ds(0, 7)], come.at[PIECE])

    for q in range(4):
        grad[rows_at(q, 3, 3), q * 128 : (q + 1) * 128] = jnp.concatenate([pieces[2 * q], pieces[2 * q + 1]], axis=0)
    near_grads, far_grads = {}, {}

    def forward_grad(s):
        if s < 3:
            wait_bytes(grad.at[pl.ds(0, 32)], come.at[NEAR_GRAD + s])
        for q in range(4):
            part = grad.at[rows_at(q, 3, s), q * 128 : (q + 1) * 128]
            for e in range(3):
                far_grads[q, e, s] = copy_to(
                    part, part, sent.at[GRAD], come.at[GRAD], chip_of(q, e)
                )
                far_grads[q, e, s].start()

    for q in range(4):
        part = grad.at[rows_at(q, 3, 3), q * 128 : (q + 1) * 128]
        for e in range(3):
            near_grads[q, e] = copy_to(
                part, part, sent.at[NEAR_GRAD + e], come.at[NEAR_GRAD + e], chip_of((q + 2) % 4, e)
            )
            near_grads[q, e].start()
    forward_grad(3)
    for s in (1, 2, 0):
        forward_grad(s)
    wait_bytes(planes.at[pl.ds(0, 3)], come.at[PLANE])
    for r in range(4):

        def lay(slot, carry):
            bit = [rem(div(slot, 1 << ((d - r) % 4)), 2) for d in range(4)]
            quarter = bit[2] * 2 + bit[3]
            for b in range(2):
                for a in range(2):
                    first = pl.multiple_of((a * 8 + 2 * r + b) * 32 + bit[1] * 16, 16)
                    old_full[bit[0], quarter, pl.ds(first, 16), :] = planes[r, slot, b, a]
            return carry

        lax.fori_loop(0, 16, lay, 0)

    wait_bytes(grad.at[pl.ds(0, 384)], come.at[GRAD])

    def eye_of(m):
        row = lax.broadcasted_iota(jnp.int32, (128, 512), 0) + m * 128
        return (row == lax.broadcasted_iota(jnp.int32, (128, 512), 1)).astype(F32)

    def flip(m, carry):
        rows = pl.ds(pl.multiple_of(m * 128, 128), 128)
        grad_t[rows, :] = grad[:, rows].T
        return carry

    lax.fori_loop(0, 4, flip, 0, unroll=True)

    def gram(m, carry):
        rows = pl.ds(pl.multiple_of(m * 128, 128), 128)
        eye = eye_of(m)
        sums_now = []
        for chain in range(2):
            one, two = (grad_t, grad) if chain == 0 else (grad, grad_t)
            term = dot(one[rows, :], two[...])
            quarters = [old_full[chain, q, rows, :] for q in range(4)]
            value = jnp.concatenate(quarters, axis=1) + term
            new_full[chain, rows, :] = value
            damped = value + DAMPING * eye
            sums_now.append(carry[chain] + jnp.sum(damped * damped, axis=0, keepdims=True))
        return tuple(sums_now)

    zero = jnp.zeros((1, 512), F32)
    squares = lax.fori_loop(0, 4, gram, (zero, zero), unroll=True)
    own_first = pl.multiple_of(z_lo * 32 + 16 * core, 16)
    other_first = pl.multiple_of(z_lo * 32 + 16 * other, 16)
    outs, sends = [], []
    for chain in range(2):
        outs.append(
            pltpu.make_async_copy(
                new_full.at[chain, pl.ds(own_first, 16)], stats.at[2 * chain + tile], here.at[4]
            )
        )
        sends.append(
            copy_to(
                new_full.at[chain, pl.ds(other_first, 16)], stats.at[2 * chain + tile],
                sent.at[OUT], come.at[OUT], partner,
            )
        )
        outs[-1].start()
        sends[-1].start()

    scales = [2.5 / jnp.sqrt(jnp.sum(part, axis=1, keepdims=True)) for part in squares]
    quarters = [jnp.sqrt(jnp.sqrt(scale)) for scale in scales]

    def begin(m, carry):
        rows = pl.ds(pl.multiple_of(m * 128, 128), 128)
        eye = eye_of(m)
        for chain in range(2):
            iterate = scales[chain] * (new_full[chain, rows, :] + DAMPING * eye)
            factor0[chain, rows, :] = ((5.0 * eye - iterate) * 0.25).astype(BF16)
            high = iterate.astype(BF16)
            left[chain, rows, :512] = high
            left[chain, rows, 512:] = (iterate - high.astype(F32)).astype(BF16)
        return carry

    lax.fori_loop(0, 4, begin, 0, unroll=True)

    def pieces_of(value):
        high = value.astype(BF16)
        return high, (value - high.astype(F32)).astype(BF16)

    def product(a, a_high, chain):
        return dot(a, right[chain, :1024, :]) + dot(a_high, right[chain, 1024:, :])

    def keep_right(chain, high, low):
        right[chain, :512, :] = high
        right[chain, 512:1024, :] = high
        right[chain, 1024:, :] = low

    for chain in range(2):
        high, low = pieces_of(dot(factor0[chain], factor0[chain]))
        square[chain, :, :512] = high
        square[chain, :, 512:] = low
        keep_right(chain, high, low)
    for chain in range(2):
        keep_right(chain, *pieces_of(product(square[chain], square[chain, :, :512], chain)))

    row_ids = lax.broadcasted_iota(jnp.int32, (256, 512), 0)
    column_ids = lax.broadcasted_iota(jnp.int32, (256, 512), 1)
    for top in range(2):
        rows = slice(256 * top, 256 * top + 256)
        eye = (row_ids + 256 * top == column_ids).astype(F32)
        for chain in range(2):
            iterate = product(left[chain, rows, :], left[chain, rows, :512], chain)
            factor1[chain, rows, :] = ((5.0 * eye - iterate) * 0.25).astype(BF16)

    chip_rows = pl.ds(pl.multiple_of(z_lo * 32, 32), 32)
    right_root = (quarters[1] * dot(factor0[1, chip_rows, :], factor1[1])).astype(BF16)
    for top in range(2):
        rows = slice(256 * top, 256 * top + 256)
        root[rows, :] = (quarters[0] * dot(factor0[0, rows, :], factor1[0])).astype(BF16)
    inner = dot(right_root, grad[...])
    high = inner.astype(BF16)
    rest = inner - high.astype(F32)
    middle = rest.astype(BF16)
    low = (rest - middle.astype(F32)).astype(BF16)
    total = dot(jnp.concatenate([low, middle, high], axis=0), root[...])
    total = (total[:32] + total[32:64]) + total[64:]
    upd[...] = total * math.sqrt(512)
    outs.append(
        pltpu.make_async_copy(
            upd.at[pl.ds(pl.multiple_of(16 * core, 16), 16)], update.at[tile], here.at[4]
        )
    )
    sends.append(
        copy_to(
            upd.at[pl.ds(pl.multiple_of(16 * other, 16), 16)], update.at[tile],
            sent.at[OUT], come.at[OUT], partner,
        )
    )
    outs[-1].start()
    sends[-1].start()

    wait_bytes(new_full.at[0, pl.ds(0, 48)], here.at[4])
    for sems in (come, sent):
        wait_bytes(new_full.at[0, pl.ds(0, 48)], sems.at[OUT])
    for t in range(2):
        wait_bytes(og_v.at[1], sent.at[SWAP + t])
    wait_bytes(old_v.at[0], sent.at[OLD])
    for s in range(4):
        wait_bytes(got0.at[s], sent.at[SUM + s])
    wait_bytes(got1, sent.at[MID])
    wait_bytes(parts, sent.at[PART])
    wait_bytes(blocks.at[pl.ds(0, 3)], sent.at[BLOCK])
    wait_bytes(pieces.at[pl.ds(0, 7)], sent.at[PIECE])
    for e in range(3):
        wait_bytes(grad.at[pl.ds(0, 32)], sent.at[NEAR_GRAD + e])
        wait_bytes(planes.at[0, pl.ds(0, 4)], sent.at[NEAR_PLANE + e])
    wait_bytes(grad.at[pl.ds(0, 384)], sent.at[GRAD])
    wait_bytes(old_full.at[0, 0, pl.ds(0, 240)], sent.at[COLUMN])
    wait_bytes(planes.at[pl.ds(0, 3)], sent.at[PLANE])


def write(stats, update, stats_out, update_out, sem):
    copies = [
        pltpu.make_async_copy(stats, stats_out, sem.at[0]),
        pltpu.make_async_copy(update, update_out, sem.at[1]),
    ]
    for copy in copies:
        copy.start()
    for copy in copies:
        copy.wait()


def on_device(activations, out_grads, stats_old):
    dma = pltpu.SemaphoreType.DMA
    vmem = pltpu.VMEM
    anywhere = pl.BlockSpec(memory_space=pl.ANY)
    results = pl.pallas_call(
        kernel,
        out_shape=(
            pltpu.VMEM((4, 16, 512), F32),
            pltpu.VMEM((2, 16, 512), F32),
        ),
        in_specs=[anywhere] * 3,
        out_specs=(pl.BlockSpec(memory_space=pltpu.VMEM),) * 2,
        scratch_shapes=[
            vmem((2, 512, 512), BF16),
            vmem((2, 512, 512), BF16),
            vmem((2, 2, 16, 512), F32),
            vmem((4, 512, 128), F32),
            vmem((4, 4, 3, 32, 128), F32),
            vmem((4, 3, 32, 128), F32),
            vmem((8, 16, 128), F32),
            vmem((7, 16, 128), F32),
            vmem((4, 16, 128), F32),
            vmem((8, 16, 128), BF16),
            vmem((512, 512), BF16),
            vmem((512, 512), BF16),
            vmem((8, 2, 16, 128), F32),
            vmem((4, 16, 2, 2, 16, 128), F32),
            vmem((2, 4, 512, 128), F32),
            vmem((2, 512, 512), F32),
            vmem((2, 512, 512), BF16),
            vmem((2, 512, 512), BF16),
            vmem((2, 512, 1024), BF16),
            vmem((2, 512, 1024), BF16),
            vmem((2, 1536, 512), BF16),
            vmem((512, 512), BF16),
            vmem((32, 512), F32),
            dma((5,)),
            dma((21,)),
            dma((21,)),
            pltpu.SemaphoreType.REGULAR((4,)),
        ],
        compiler_params=pltpu.CompilerParams(
            collective_id=0, has_side_effects=True, vmem_limit_bytes=56 * 1024 * 1024
        ),
    )(activations, out_grads, stats_old)
    return pl.pallas_call(
        write,
        out_shape=(
            jax.ShapeDtypeStruct((4, 16, 512), F32),
            jax.ShapeDtypeStruct((2, 16, 512), F32),
        ),
        in_specs=[anywhere] * 2,
        out_specs=(anywhere, anywhere),
        scratch_shapes=[dma((2,))],
    )(*[pltpu.with_memory_space_constraint(result, pltpu.VMEM) for result in results])


def solution(mesh):
    in_specs = (P(("rep", "grp"), None), P(("rep", "grp"), None), P(None, "grp", None))
    out_specs = (P(None, "grp", None), P(None, "grp", None))
    return jax.shard_map(
        on_device, mesh=mesh, in_specs=in_specs, out_specs=out_specs, check_vma=False
    )
```

```python
import functools
import math

import jax
import jax.numpy as jnp
from jax import lax
from jax.experimental import pallas as pl
from jax.experimental.pallas import tpu as pltpu
from jax.sharding import PartitionSpec as P

MESH = pl.DeviceIdType.MESH
F32 = jnp.float32
BF16 = jnp.bfloat16
DAMPING = 0.01
ITERS = 2


SWAP, OLD, SUM, MID, PART, BLOCK, NEAR_GRAD, GRAD, COLUMN, NEAR_PLANE, PLANE, OUT = (
    0, 2, 3, 7, 8, 9, 10, 14, 15, 16, 19, 20
)


def wait_bytes(ref, sem):
    pltpu.make_async_copy(ref, ref, sem).wait()


def div(a, b):
    return lax.div(a, jnp.int32(b))


def rem(a, b):
    return lax.rem(a, jnp.int32(b))


def dot(a, b):
    return jnp.dot(a, b, preferred_element_type=F32)


def transposed_dot(a, b):
    return lax.dot_general(a, b, (((0,), (0,)), ((), ())), preferred_element_type=F32)


def copy_to(src, dst, send, recv, device):
    return pltpu.make_async_remote_copy(
        src_ref=src, dst_ref=dst, send_sem=send, recv_sem=recv, device_id=device, device_id_type=MESH
    )


def kernel(
    act, og, old, stats, update,
    act_v, og_v, old_v, acc, got0, got1, shard, parts, blocks, pieces, grad, grad_t,
    column, planes, old_full, new_full, factor0, factor1, left, square, right, root, upd,
    here, sent, come, know,
):
    rep, grp = lax.axis_index("rep"), lax.axis_index("grp")
    z_hi, xy = rem(rep, 2), div(rep, 2)
    y, x = rem(xy, 4), div(xy, 4)
    core, z_lo = rem(grp, 2), div(grp, 2)
    z = z_hi * 16 + z_lo
    blk, pos = div(z, 8), rem(z, 8)
    other = 1 - core
    tile = rem(core + (x + y + z), 2)
    other_tile = 1 - tile

    def device(x_at, y_at, z_at, tile_at):
        core_at = rem(tile_at + (x_at + y_at + z_at), 2)
        return {"rep": (x_at * 4 + y_at) * 2 + div(z_at, 16), "grp": rem(z_at, 16) * 2 + core_at}

    def along(k):
        return device(x, y, rem(z + (k + 32), 32), tile)

    partner = device(x, y, z, other_tile)
    x_at = [x + 1 - 2 * rem(x, 2), 3 - x]
    y_at = [y + 1 - 2 * rem(y, 2), 3 - y]
    bits = [rem(rem(x, 2) + div(x, 2), 2), rem(rem(y, 2) + div(y, 2), 2), div(x, 2), div(y, 2)]
    hops = [device(x_at[0], y, z, tile), device(x, y_at[0], z, tile), device(x_at[1], y, z, tile), device(x, y_at[1], z, tile)]
    across = [
        device(x_at[0], y_at[0], z, tile),
        device(x_at[1], y_at[0], z, tile),
        device(x_at[1], y_at[1], z, tile),
        device(x_at[0], y_at[1], z, tile),
    ]

    def chip_of(d, e):
        return (across[d], hops[d], hops[(d + 1) % 4])[e]

    def place_of(d, e):
        flip_x, flip_y = (e in (0, 1), e in (0, 2)) if d % 2 == 0 else (e in (0, 2), e in (0, 1))
        along_x, along_y = (d // 2, d // 2) if d % 2 == 0 else ((d + 1) % 4 // 2, d // 2)
        return (x_at[along_x] if flip_x else x), (y_at[along_y] if flip_y else y)

    def number_of(d, e):
        first, second = bits[d], bits[(d + 1) % 4]
        if e in (0, 1):
            first = 1 - first
        if e in (0, 2):
            second = 1 - second
        return first * 2 + second

    barrier = pltpu.get_barrier_semaphore()
    for near in [partner, *hops, *across, along(1), along(-1)]:
        pl.semaphore_signal(barrier, inc=1, device_id=near, device_id_type=MESH)

    own_cols = pl.ds(pl.multiple_of(tile * 512, 512), 512)
    other_cols = pl.ds(pl.multiple_of(other_tile * 512, 512), 512)
    loads = [
        pltpu.make_async_copy(act, act_v.at[0], here.at[0]),
        pltpu.make_async_copy(og.at[:, own_cols], og_v.at[0], here.at[0]),
        pltpu.make_async_copy(old.at[tile], old_v.at[core, 0], here.at[1]),
        pltpu.make_async_copy(old.at[tile + 2], old_v.at[core, 1], here.at[1]),
    ]
    for load in loads:
        load.start()

    pl.semaphore_wait(barrier, 11)

    def spread(k):
        for far in (along(1 << k), along(-(1 << k))):
            pl.semaphore_signal(know.at[k], inc=1, device_id=far, device_id_type=MESH)

    swaps = []
    for t in range(2):
        half_rows = slice(256 * t, 256 * t + 256)
        pair = sent.at[SWAP + t], come.at[SWAP + t], partner
        swaps += [
            copy_to(og.at[half_rows, other_cols], og_v.at[1, half_rows], *pair),
            copy_to(act.at[half_rows], act_v.at[1, half_rows], *pair),
        ]
    pair = sent.at[OLD], come.at[OLD], partner
    swaps += [
        copy_to(old.at[other_tile], old_v.at[core, 0], *pair),
        copy_to(old.at[other_tile + 2], old_v.at[core, 1], *pair),
    ]
    for swap in swaps:
        swap.start()
    spread(0)

    def local_term(side, first, count, add):
        for m in range(4):
            rows = slice(128 * m, 128 * m + 128)
            grad_t[rows, first : first + count] = og_v[side, first : first + count, rows].T
        term = dot(grad_t[:, first : first + count], act_v[side, first : first + count])
        for q in range(4):
            value = term[:, q * 128 : (q + 1) * 128]
            acc[q] = acc[q] + value if add else value

    wait_bytes(og_v, here.at[0])
    local_term(0, 0, 512, False)
    pl.semaphore_wait(know.at[0], 2)
    spread(1)
    for t in range(2):
        wait_bytes(og_v.at[1], come.at[SWAP + t])
        local_term(1, 256 * t, 256, True)

    def rows_at(q, e, s):
        return pl.ds(pl.multiple_of(128 * number_of(q, e) + 32 * number_of((q + 2) % 4, s), 32), 32)

    sums = {}
    for s in range(4):
        for q in range(4):
            for e in range(3):
                sums[q, e, s] = copy_to(
                    acc.at[q, rows_at(q, e, s)], got0.at[s, q, e], sent.at[SUM + s], come.at[SUM + s], chip_of(q, e)
                )
                sums[q, e, s].start()
    wait_bytes(old_v.at[0], here.at[1])
    wait_bytes(old_v.at[0], come.at[OLD])

    slice_cols = pl.ds(pl.multiple_of((bits[2] * 2 + bits[3]) * 128, 128), 128)
    mine = old_v.at[bits[1], bits[0], :, slice_cols]
    half = div(z_lo, 8)
    stage = pltpu.make_async_copy(mine, column.at[pos, half], here.at[2])
    stage.start()
    pl.semaphore_wait(know.at[1], 2)
    spread(2)

    def take_sum(q, s):
        return (acc[q, rows_at(q, 3, s), :] + got0[s, q, 0]) + (got0[s, q, 1] + got0[s, q, 2])

    mids = {}
    columns = []
    for s in range(3):
        wait_bytes(got0.at[s], come.at[SUM + s])
        for q in range(4):
            acc[q, rows_at(q, 3, s), :] = take_sum(q, s)
            mids[q, s] = copy_to(
                acc.at[q, rows_at(q, 3, s)], got1.at[q, s], sent.at[MID], come.at[MID], chip_of((q + 2) % 4, s)
            )
            mids[q, s].start()
        if s == 0:
            stage.wait()
            pl.semaphore_wait(know.at[2], 2)
            spread(3)
            for i, k in enumerate([8, -7, 7, -6, 6, -5, 5, -4, 4, -3, 3, -2, 2, -1, 1]):
                copy = copy_to(mine, column.at[pos, half], sent.at[COLUMN], come.at[COLUMN], along(k))
                copy.start()
                columns.append(copy)
    wait_bytes(got0.at[3], come.at[SUM + 3])
    wait_bytes(got1, come.at[MID])
    for q in range(4):
        value = take_sum(q, 3)
        value = value + ((got1[q, 0] + got1[q, 1]) + got1[q, 2])
        for h in range(2):
            shard[2 * q + h] = value[16 * h : 16 * h + 16]

    around = [-4, 3, -3, 2, -2, 1, -1]
    to_parts = []
    for i, k in enumerate(around):
        copy = copy_to(
            shard.at[rem(pos + (k + 8), 8)], parts.at[i], sent.at[PART], come.at[PART], along(k)
        )
        copy.start()
        to_parts.append(copy)

    wait_bytes(old_full.at[0, 0, pl.ds(0, 240)], come.at[COLUMN])

    number = bits[0] + 2 * bits[1] + 4 * bits[2] + 8 * bits[3]
    slots = [div(number, 1 << r) + rem(number, 1 << r) * (1 << (4 - r)) for r in range(4)]
    stages = [
        pltpu.make_async_copy(column.at[pl.ds(2 * r, 2)], planes.at[r, slots[r]], here.at[3])
        for r in range(4)
    ]
    for copy in stages:
        copy.start()
    wait_bytes(planes.at[0, pl.ds(0, 4)], here.at[3])
    near_planes, far_planes = {}, {}

    def slots_at(r, e):
        flip = number_of(r, e)
        first, second = div(flip, 2), rem(flip, 2)
        return slots[r] - rem(slots[r], 4) + first + 2 * second

    def forward_plane(s):
        if s < 3:
            wait_bytes(planes.at[0, pl.ds(0, 4)], come.at[NEAR_PLANE + s])
        for r in range(4):
            at = slots_at(r, s)
            for e in range(3):
                far_planes[r, e, s] = copy_to(
                    planes.at[r, at], planes.at[r, at], sent.at[PLANE], come.at[PLANE], chip_of((r + 2) % 4, e)
                )
                far_planes[r, e, s].start()

    for r in range(4):
        for e in range(3):
            near_planes[r, e] = copy_to(
                planes.at[r, slots[r]], planes.at[r, slots[r]], sent.at[NEAR_PLANE + e], come.at[NEAR_PLANE + e], chip_of(r, e)
            )
            near_planes[r, e].start()
    forward_plane(3)

    total = shard[pos]
    for i in range(7):
        if i == 0:
            wait_bytes(parts, come.at[PART])
        total = total + parts[i]
    blocks[blk] = total
    pl.semaphore_wait(know.at[3], 2)
    to_blocks = []
    for k in range(1, 4):
        copy = copy_to(
            blocks.at[blk], blocks.at[blk], sent.at[BLOCK], come.at[BLOCK], along(8 * k)
        )
        copy.start()
        to_blocks.append(copy)

    for s in (1, 2, 0):
        forward_plane(s)

    wait_bytes(blocks.at[pl.ds(0, 3)], come.at[BLOCK])
    pieces[...] = (((blocks[0] + blocks[1]) + blocks[2]) + blocks[3]).astype(BF16)
    quarter_at = div(pos, 2)

    n = quarter_at
    picks = [
        div((1 - n) * (2 - n) * (3 - n), 6), div(n * (2 - n) * (3 - n), 2), div(n * (n - 1) * (3 - n), 2), div(n * (n - 1) * (n - 2), 6)
    ]

    def choose(values):
        return sum(pick * value for pick, value in zip(picks, values))

    piece_first = choose([128 * number_of(q, 3) + 32 * number_of((q + 2) % 4, 3) for q in range(4)]) + 16 * rem(pos, 2)
    piece_at = grad.at[
        pl.ds(pl.multiple_of(piece_first, 16), 16), pl.ds(pl.multiple_of(quarter_at * 128, 128), 128)
    ]
    for e in (0, 3, 1, 2):
        for k in (-4, 3, -3, 2, -2, 1, -1, 0):
            if e == 3 and k == 0:
                continue
            z_to = rem(z + (k + 32), 32)
            to_x = choose([place_of((q + 2) % 4, e)[0] for q in range(4)])
            to_y = choose([place_of((q + 2) % 4, e)[1] for q in range(4)])
            copy_to(pieces, piece_at, sent.at[NEAR_GRAD + e], come.at[NEAR_GRAD + e], device(to_x, to_y, z_to, tile)).start()
    keep_piece = pltpu.make_async_copy(pieces, piece_at, here.at[2])
    keep_piece.start()
    far_grads = {}

    def forward_grad(s):
        wait_bytes(old_full.at[0, 0, pl.ds(0, 56 if s == 3 else 64)], come.at[NEAR_GRAD + s])
        for q in range(4):
            part = grad.at[rows_at(q, 3, s), q * 128 : (q + 1) * 128]
            for e in range(3):
                far_grads[q, e, s] = copy_to(
                    part, part, sent.at[GRAD], come.at[GRAD], chip_of(q, e)
                )
                far_grads[q, e, s].start()

    keep_piece.wait()
    for s in (3, 1, 2, 0):
        forward_grad(s)
    wait_bytes(planes.at[pl.ds(0, 3)], come.at[PLANE])
    for r in range(4):

        def lay(slot, carry):
            bit = [rem(div(slot, 1 << ((d - r) % 4)), 2) for d in range(4)]
            quarter = bit[2] * 2 + bit[3]
            for b in range(2):
                for a in range(2):
                    first = pl.multiple_of((a * 8 + 2 * r + b) * 32 + bit[1] * 16, 16)
                    old_full[bit[0], quarter, pl.ds(first, 16), :] = planes[r, slot, b, a]
            return carry

        lax.fori_loop(0, 16, lay, 0)

    wait_bytes(grad.at[pl.ds(0, 384)], come.at[GRAD])

    def eye_of(m):
        row = lax.broadcasted_iota(jnp.int32, (128, 512), 0) + m * 128
        return (row == lax.broadcasted_iota(jnp.int32, (128, 512), 1)).astype(F32)

    def flip(m, carry):
        rows = pl.ds(pl.multiple_of(m * 128, 128), 128)
        grad_t[rows, :] = grad[:, rows].T
        return carry

    lax.fori_loop(0, 4, flip, 0, unroll=True)

    def gram(m, carry):
        rows = pl.ds(pl.multiple_of(m * 128, 128), 128)
        eye = eye_of(m)
        sums_now = []
        for chain in range(2):
            one, two = (grad_t, grad) if chain == 0 else (grad, grad_t)
            term = dot(one[rows, :], two[...])
            quarters = [old_full[chain, q, rows, :] for q in range(4)]
            value = jnp.concatenate(quarters, axis=1) + term
            new_full[chain, rows, :] = value
            damped = value + DAMPING * eye
            sums_now.append(carry[chain] + jnp.sum(damped * damped, axis=0, keepdims=True))
        return tuple(sums_now)

    zero = jnp.zeros((1, 512), F32)
    squares = lax.fori_loop(0, 4, gram, (zero, zero), unroll=True)
    own_first = pl.multiple_of(z_lo * 32 + 16 * core, 16)
    other_first = pl.multiple_of(z_lo * 32 + 16 * other, 16)
    outs, sends = [], []
    for chain in range(2):
        outs.append(
            pltpu.make_async_copy(
                new_full.at[chain, pl.ds(own_first, 16)], stats.at[2 * chain + tile], here.at[4]
            )
        )
        sends.append(
            copy_to(
                new_full.at[chain, pl.ds(other_first, 16)], stats.at[2 * chain + tile],
                sent.at[OUT], come.at[OUT], partner,
            )
        )
        outs[-1].start()
        sends[-1].start()

    scales = [2.5 / jnp.sqrt(jnp.sum(part, axis=1, keepdims=True)) for part in squares]
    quarters = [jnp.sqrt(jnp.sqrt(scale)) for scale in scales]

    def begin(m, carry):
        rows = pl.ds(pl.multiple_of(m * 128, 128), 128)
        eye = eye_of(m)
        for chain in range(2):
            iterate = scales[chain] * (new_full[chain, rows, :] + DAMPING * eye)
            factor0[chain, rows, :] = ((5.0 * eye - iterate) * 0.25).astype(BF16)
            high = iterate.astype(BF16)
            left[chain, rows, :512] = high
            left[chain, rows, 512:] = (iterate - high.astype(F32)).astype(BF16)
        return carry

    lax.fori_loop(0, 4, begin, 0, unroll=True)

    def pieces_of(value):
        high = value.astype(BF16)
        return high, (value - high.astype(F32)).astype(BF16)

    def product(a, a_high, chain):
        return dot(a, right[chain, :1024, :]) + dot(a_high, right[chain, 1024:, :])

    def keep_right(chain, high, low):
        right[chain, :512, :] = high
        right[chain, 512:1024, :] = high
        right[chain, 1024:, :] = low

    for chain in range(2):
        high, low = pieces_of(dot(factor0[chain], factor0[chain]))
        square[chain, :, :512] = high
        square[chain, :, 512:] = low
        keep_right(chain, high, low)
    for chain in range(2):
        keep_right(chain, *pieces_of(product(square[chain], square[chain, :, :512], chain)))

    row_ids = lax.broadcasted_iota(jnp.int32, (256, 512), 0)
    column_ids = lax.broadcasted_iota(jnp.int32, (256, 512), 1)
    for top in range(2):
        rows = slice(256 * top, 256 * top + 256)
        eye = (row_ids + 256 * top == column_ids).astype(F32)
        for chain in range(2):
            iterate = product(left[chain, rows, :], left[chain, rows, :512], chain)
            factor1[chain, rows, :] = ((5.0 * eye - iterate) * 0.25).astype(BF16)

    chip_rows = pl.ds(pl.multiple_of(z_lo * 32, 32), 32)
    right_root = (quarters[1] * dot(factor0[1, chip_rows, :], factor1[1])).astype(BF16)
    for top in range(2):
        rows = slice(256 * top, 256 * top + 256)
        root[rows, :] = (quarters[0] * dot(factor0[0, rows, :], factor1[0])).astype(BF16)
    inner = dot(right_root, grad[...])
    high = inner.astype(BF16)
    rest = inner - high.astype(F32)
    middle = rest.astype(BF16)
    low = (rest - middle.astype(F32)).astype(BF16)
    total = dot(jnp.concatenate([low, middle, high], axis=0), root[...])
    total = (total[:32] + total[32:64]) + total[64:]
    upd[...] = total * math.sqrt(512)
    outs.append(
        pltpu.make_async_copy(
            upd.at[pl.ds(pl.multiple_of(16 * core, 16), 16)], update.at[tile], here.at[4]
        )
    )
    sends.append(
        copy_to(
            upd.at[pl.ds(pl.multiple_of(16 * other, 16), 16)], update.at[tile],
            sent.at[OUT], come.at[OUT], partner,
        )
    )
    outs[-1].start()
    sends[-1].start()

    wait_bytes(new_full.at[0, pl.ds(0, 48)], here.at[4])
    for sems in (come, sent):
        wait_bytes(new_full.at[0, pl.ds(0, 48)], sems.at[OUT])
    for t in range(2):
        wait_bytes(og_v.at[1], sent.at[SWAP + t])
    wait_bytes(old_v.at[0], sent.at[OLD])
    for s in range(4):
        wait_bytes(got0.at[s], sent.at[SUM + s])
    wait_bytes(got1, sent.at[MID])
    wait_bytes(parts, sent.at[PART])
    wait_bytes(blocks.at[pl.ds(0, 3)], sent.at[BLOCK])
    wait_bytes(old_full.at[0, 0, pl.ds(0, 56)], sent.at[NEAR_GRAD + 3])
    for e in range(3):
        wait_bytes(grad.at[pl.ds(0, 32)], sent.at[NEAR_GRAD + e])
        wait_bytes(planes.at[0, pl.ds(0, 4)], sent.at[NEAR_PLANE + e])
    wait_bytes(grad.at[pl.ds(0, 384)], sent.at[GRAD])
    wait_bytes(old_full.at[0, 0, pl.ds(0, 240)], sent.at[COLUMN])
    wait_bytes(planes.at[pl.ds(0, 3)], sent.at[PLANE])


def write(stats, update, stats_out, update_out, sem):
    copies = [
        pltpu.make_async_copy(stats, stats_out, sem.at[0]),
        pltpu.make_async_copy(update, update_out, sem.at[1]),
    ]
    for copy in copies:
        copy.start()
    for copy in copies:
        copy.wait()


def on_device(activations, out_grads, stats_old):
    dma = pltpu.SemaphoreType.DMA
    vmem = pltpu.VMEM
    anywhere = pl.BlockSpec(memory_space=pl.ANY)
    results = pl.pallas_call(
        kernel,
        out_shape=(
            pltpu.VMEM((4, 16, 512), F32),
            pltpu.VMEM((2, 16, 512), F32),
        ),
        in_specs=[anywhere] * 3,
        out_specs=(pl.BlockSpec(memory_space=pltpu.VMEM),) * 2,
        scratch_shapes=[
            vmem((2, 512, 512), BF16),
            vmem((2, 512, 512), BF16),
            vmem((2, 2, 16, 512), F32),
            vmem((4, 512, 128), F32),
            vmem((4, 4, 3, 32, 128), F32),
            vmem((4, 3, 32, 128), F32),
            vmem((8, 16, 128), F32),
            vmem((7, 16, 128), F32),
            vmem((4, 16, 128), F32),
            vmem((16, 128), BF16),
            vmem((512, 512), BF16),
            vmem((512, 512), BF16),
            vmem((8, 2, 16, 128), F32),
            vmem((4, 16, 2, 2, 16, 128), F32),
            vmem((2, 4, 512, 128), F32),
            vmem((2, 512, 512), F32),
            vmem((2, 512, 512), BF16),
            vmem((2, 512, 512), BF16),
            vmem((2, 512, 1024), BF16),
            vmem((2, 512, 1024), BF16),
            vmem((2, 1536, 512), BF16),
            vmem((512, 512), BF16),
            vmem((32, 512), F32),
            dma((5,)),
            dma((21,)),
            dma((21,)),
            pltpu.SemaphoreType.REGULAR((4,)),
        ],
        compiler_params=pltpu.CompilerParams(
            collective_id=0, has_side_effects=True, vmem_limit_bytes=56 * 1024 * 1024
        ),
    )(activations, out_grads, stats_old)
    return pl.pallas_call(
        write,
        out_shape=(
            jax.ShapeDtypeStruct((4, 16, 512), F32),
            jax.ShapeDtypeStruct((2, 16, 512), F32),
        ),
        in_specs=[anywhere] * 2,
        out_specs=(anywhere, anywhere),
        scratch_shapes=[dma((2,))],
    )(*[pltpu.with_memory_space_constraint(result, pltpu.VMEM) for result in results])


def solution(mesh):
    in_specs = (P(("rep", "grp"), None), P(("rep", "grp"), None), P(None, "grp", None))
    out_specs = (P(None, "grp", None), P(None, "grp", None))
    return jax.shard_map(
        on_device, mesh=mesh, in_specs=in_specs, out_specs=out_specs, check_vma=False
    )
```
